512 devices in a mesh: lev: 4 (over x_lo, core), tile: 128 (over y, x_hi, z).
Axes of the slice: x: 4 (x_hi: 2, x_lo: 2; x = x_hi * 2 + x_lo), y: 4, z: 16, core: 2. Of those that a mesh axis runs over, the one named last changes fastest.
Arguments:
- forcing: bfloat16 [4, 128, 36, 36, 128], P('lev', 'tile'), may hold values from -6 to 6
- transport: float32 [4, 4, 128, 36, 36], P(None, 'lev', 'tile'), may hold values from 0.04 to 0.22
- reactivity: float32 [4, 128, 36, 36], P('lev', 'tile'), may hold values from 0.1 to 0.6
- jacobian: float32 [4, 128, 128], P('lev'), may hold values from -0.5 to 0.5
- pattern: int32 [8, 8], replicated, may hold values 0 or 1
- lon_rate: float32 [128, 576], P('tile'), may hold values from 0.003 to 0.03
- lat_rate: float32 [128, 288], P('tile'), may hold values from 0.003 to 0.03
- vertical: float32 [128, 4, 4], replicated, may hold values from -3 to 3
- step_scale: float32 [128], replicated, may hold values from 0.3 to 1
- control: bfloat16 [4, 128, 36, 36, 128], P('lev', 'tile'), may hold values from -6 to 6
Outputs:
- control_new: bfloat16 [4, 128, 36, 36, 128], P('lev', 'tile')
The draws below stay inside these ranges and needn't reach their ends.
All inputs are finite; a program needn't handle non-finite values.
Results may differ from the reference program's by a relative error of at most 0.001.
The reference program's roundings to bfloat16 on the way (of `gradient` and `filtered`) count: a program that leaves them out, or rounds other values in their place, can miss the bound.
Values may be sent and summed in bfloat16 or wider, within the bound.
No kernel may reach another device: no remote copies, remote signals or barrier semaphores. Data moves between devices by JAX's collectives and lax.ppermute only.
A program may use at most 64 MiB of HBM per device.

```python
import math
import jax
import jax.numpy as jnp
from jax import lax

S = 128
TJ = 8
STEPS = 3
TX = 36
TY = 36
LEV = 4
TILES = 128
NLON = 576
NLAT = 288
NBLK = 8


def with_ends(array, stream_key, least, largest):
    index_at = [jax.random.randint(jax.random.fold_in(stream_key, axis), (), 0, length) for axis, length in enumerate(array.shape)]
    main_axis = array.shape.index(max(array.shape))
    neighbour = index_at[:main_axis] + [(index_at[main_axis] + 1) % array.shape[main_axis]] + index_at[main_axis + 1:]
    return array.at[tuple(index_at)].set(least).at[tuple(neighbour)].set(largest)


def level_of(rng, dims, shards, smallest, largest):
    factor_of, own = 1.0, jax.random.fold_in(rng, 6)
    for dim, parts in shards:
        draws = jnp.exp(jax.random.uniform(jax.random.fold_in(own, dim), (parts,), jnp.float32, smallest / len(shards), largest / len(shards)))
        factor_of = factor_of * jnp.repeat(draws, dims[dim] // parts).reshape([-1 if axis == dim else 1 for axis in range(len(dims))])
    return factor_of


def gaussian(key, shape, deviation, reach, pieces=(), held_as=jnp.bfloat16):
    drawn = deviation * jax.random.normal(key, shape, jnp.float32)
    if pieces:
        drawn = drawn * level_of(key, shape, pieces, -0.22, 0.18)
    return jnp.clip(drawn, -reach, reach).astype(held_as)


def setup_inputs(seed: int = 0) -> dict:
    key_list = jax.random.split(jax.random.key(seed), 11)
    forcing = gaussian(key_list[0], (LEV, TILES, TX, TY, S), 1.0, 6.0, ((0, 4), (1, 128)))
    transport = jnp.clip(0.04 + 0.18 * jax.random.uniform(key_list[1], (4, LEV, TILES, TX, TY), jnp.float32) ** level_of(key_list[1], (4, LEV, TILES, TX, TY), ((1, 4), (2, 128)), -0.2, 0.2), 0.04, 0.22)
    reactivity = jnp.clip(jnp.exp(math.log(0.6) - 1.7917595 * jax.random.uniform(key_list[2], (LEV, TILES, TX, TY), jnp.float32) ** level_of(key_list[2], (LEV, TILES, TX, TY), ((0, 4), (1, 128)), -0.2, 0.2)), 0.1, 0.6)
    jacobian = gaussian(key_list[3], (LEV, S, S), S ** -0.5, 0.5, ((0, 4),), jnp.float32)
    pattern = with_ends((jax.random.randint(key_list[4], (NBLK, NBLK), 0, 2) < 1).astype(jnp.int32), jax.random.fold_in(key_list[4], 1), 0, 1)
    lon_rate = jnp.clip(jnp.exp(math.log(0.03) - 2.3025851 * jax.random.uniform(key_list[5], (S, NLON), jnp.float32) ** level_of(key_list[5], (S, NLON), ((0, 128),), -0.2, 0.2)), 0.003, 0.03)
    lat_rate = jnp.clip(jnp.exp(math.log(0.03) - 2.3025851 * jax.random.uniform(key_list[6], (S, NLAT), jnp.float32) ** level_of(key_list[6], (S, NLAT), ((0, 128),), -0.2, 0.2)), 0.003, 0.03)
    vertical = gaussian(key_list[7], (S, LEV, LEV), 0.5, 3.0, (), jnp.float32)
    step_scale = jnp.clip(jnp.exp(jax.random.uniform(key_list[8], (S,), jnp.float32, math.log(0.3), math.log(1.0))), 0.3, 1.0)
    control = gaussian(key_list[9], (LEV, TILES, TX, TY, S), 1.0, 6.0, ((0, 4), (1, 128)))
    return {"forcing": forcing, "transport": transport, "reactivity": reactivity, "jacobian": jacobian, "pattern": pattern, "lon_rate": lon_rate, "lat_rate": lat_rate, "vertical": vertical, "step_scale": step_scale, "control": control}


def to_grid(values):
    lon_tiles = values.shape[0] // TJ
    shaped = values.reshape((lon_tiles, TJ) + values.shape[1:])
    shaped = jnp.swapaxes(shaped, 1, 2)
    return shaped.reshape((lon_tiles * values.shape[1], TJ * values.shape[2]) + values.shape[3:])

def to_tiles(values, tile_rows, tile_cols):
    lon_tiles = values.shape[0] // tile_rows
    shaped = values.reshape((lon_tiles, tile_rows, TJ, tile_cols) + values.shape[2:])
    shaped = jnp.swapaxes(shaped, 1, 2)
    return shaped.reshape((lon_tiles * TJ, tile_rows, tile_cols) + values.shape[2:])

def exp_filter(values, rates):
    rates_line = rates.T
    quarter = jnp.sqrt(jnp.sqrt(rates_line))
    scaled = values * quarter[:, None, :]
    decay = jnp.exp(-rates_line)
    decay_after = jnp.concatenate([decay[1:], jnp.zeros_like(decay[:1])], 0)

    def forward(carry, inputs):
        item, factor = inputs
        carry = item + factor[None, :] * carry
        return (carry, carry)
    anchor = jnp.zeros(values.shape[1:], values.dtype)
    _, ahead = lax.scan(forward, anchor, (scaled, decay))
    _, behind = lax.scan(forward, anchor, (scaled, decay_after), reverse=True)
    return quarter[:, None, :] * (ahead + behind - scaled)

def reference(forcing, transport, reactivity, jacobian, pattern, lon_rate, lat_rate, vertical, step_scale, control):
    groups = pattern.shape[0]
    width = S // groups
    blockmask = jnp.broadcast_to(pattern.astype(jnp.float32)[:, None, :, None], (groups, width, groups, width)).reshape(S, S)

    def one_level(inputs):
        forcing_level, transport_level, reactivity_level, jacobian_level = inputs
        adjoint = to_grid(forcing_level).astype(jnp.float32)
        weights = [to_grid(transport_level[k])[:, :, None] for k in range(4)]
        reacting = to_grid(reactivity_level)[:, :, None]
        coupling = jacobian_level * blockmask
        for sweep in range(STEPS):
            from_west = jnp.roll(adjoint, 1, axis=0)
            from_east = jnp.roll(adjoint, -1, axis=0)
            zero_column = jnp.zeros_like(adjoint[:, :1])
            from_south = jnp.concatenate([zero_column, adjoint[:, :-1]], 1)
            from_north = jnp.concatenate([adjoint[:, 1:], zero_column], 1)
            moved = adjoint + weights[0] * (from_west - adjoint) + weights[1] * (from_east - adjoint) + weights[2] * (from_south - adjoint) + weights[3] * (from_north - adjoint)
            reacted = jnp.dot(moved.reshape(-1, S), coupling, precision=lax.Precision.HIGHEST, preferred_element_type=jnp.float32)
            adjoint = moved + reacting * reacted.reshape(moved.shape)
        gradient = lax.optimization_barrier(adjoint.astype(jnp.bfloat16)).astype(jnp.float32)
        along_lon = exp_filter(gradient, lon_rate)
        along_lat = exp_filter(jnp.swapaxes(along_lon, 0, 1), lat_rate)
        filtered = jnp.swapaxes(along_lat, 0, 1).astype(jnp.bfloat16)
        return to_tiles(filtered, TX, TY)
    filtered_all = lax.map(one_level, (forcing, jnp.moveaxis(transport, 1, 0), reactivity, jacobian))

    def update_level(inputs):
        level, control_level = inputs
        mixing = vertical[:, level, :]
        total = jnp.zeros(control_level.shape, jnp.float32)
        for other in range(LEV):
            total = total + mixing[:, other] * filtered_all[other].astype(jnp.float32)
        return (control_level.astype(jnp.float32) - step_scale * total).astype(jnp.bfloat16)
    return lax.map(update_level, (jnp.arange(LEV, dtype=jnp.int32), control))
```

```python
import jax
import jax.numpy as jnp
import numpy as np
from jax import lax
from jax.experimental import pallas as pl
from jax.experimental.pallas import tpu as pltpu
from jax.sharding import PartitionSpec as P

TJ = 8
TI = 16
STEPS = 3
NX = 36
NY = 36
S = 128
YP = 48
Y0 = 8
YO = 40
NXE = NX + 6
FLD = 5
HIGHEST = lax.Precision.HIGHEST
VMEM = pl.BlockSpec(memory_space=pltpu.VMEM)
LON_MASKS = (8, 16, 32, 64)
LAT_MASKS = (1, 2, 4)


def scan_tables(count):
    bits = count.bit_length() - 1
    masks = np.zeros((count, 6 * bits, count), np.float32)
    gates = np.ones((count, 6 * bits, 1), np.float32)
    tiles = np.arange(count)
    for me in range(count):
        for k in range(bits):
            bit = (me >> k) & 1
            own = ((tiles >> k) == (me >> k)).astype(np.float32)
            other = ((tiles >> k) == ((me >> k) ^ 1)).astype(np.float32)
            none = np.zeros_like(own)
            masks[me, 6 * k + 0] = none if bit else other
            masks[me, 6 * k + 1] = own if bit else none
            masks[me, 6 * k + 2] = other if bit else none
            masks[me, 6 * k + 3] = none if bit else own
            masks[me, 6 * k + 4] = own * (tiles < me)
            masks[me, 6 * k + 5] = own * (tiles > me)
            gates[me, 6 * k + 4] = bit
            gates[me, 6 * k + 5] = 1 - bit
    return masks, gates


def tables_kernel(rate_ref, lonm_ref, latm_ref, long_ref, latg_ref, lon_ref, lat_ref, lonc_ref, latc_ref):
    fields = rate_ref[...].T
    row = lax.broadcasted_iota(jnp.int32, (YO, YO), 0)
    col = lax.broadcasted_iota(jnp.int32, (YO, YO), 1)
    upto = (col <= row).astype(jnp.float32)
    after = (col > row).astype(jnp.float32)
    for first, out in ((0, lon_ref), (YO, lat_ref)):
        rates = fields[first : first + YO]
        quarter = jnp.sqrt(jnp.sqrt(rates))
        ahead = jnp.dot(upto, rates, precision=HIGHEST, preferred_element_type=jnp.float32)
        behind = jnp.dot(after, rates, precision=HIGHEST, preferred_element_type=jnp.float32)
        out[0] = jnp.exp(-rates)
        out[1] = quarter
        out[2] = quarter * jnp.exp(-ahead)
        out[3] = quarter * jnp.exp(-behind)
    for first, size, mask, gate, out in (
        (2 * YO, TI, lonm_ref, long_ref, lonc_ref),
        (2 * YO + TI, TJ, latm_ref, latg_ref, latc_ref),
    ):
        total = jnp.dot(
            mask[...], fields[first : first + size], precision=HIGHEST, preferred_element_type=jnp.float32
        )
        out[...] = gate[...] * jnp.exp(-total)


def steps_kernel(
    forcing_ref, south_ref, north_ref, west_ref, east_ref, planes_ref, coupling_ref, lon_ref,
    local_ref, edge_ref, state, moved, weights,
):
    state[...] = jnp.zeros_like(state)
    for side, line in ((west_ref, 0), (east_ref, NX + 3)):
        for i in range(3):
            at = (line + i + 1) * YP + Y0 - 2
            state[at : at + NY + 4, :] = side[i].astype(jnp.float32)

    def place(x, carry):
        at = pl.multiple_of((x + 4) * YP + Y0, 8)
        state[pl.ds(at, NY), :] = forcing_ref[x].astype(jnp.float32)
        return carry

    lax.fori_loop(0, NX, place, 0)
    for j in range(3):
        state[pl.ds(4 * YP + Y0 - 3 + j, NX, stride=YP), :] = south_ref[j].astype(jnp.float32)
        state[pl.ds(4 * YP + Y0 + NY + j, NX, stride=YP), :] = north_ref[j].astype(jnp.float32)
    for f in range(FLD):
        column = planes_ref[f].T
        for x in range(NXE):
            weights[f, x * YP : (x + 1) * YP, :] = jnp.broadcast_to(column[:YP, x : x + 1], (YP, S))

    def transport_line(x, carry):
        at = pl.multiple_of(x * YP, 8)
        here = state[pl.ds(at + YP, YP), :]
        west = state[pl.ds(at, YP), :]
        east = state[pl.ds(at + 2 * YP, YP), :]
        south = pltpu.roll(here, 1, 0)
        north = pltpu.roll(here, YP - 1, 0)
        line = pl.ds(at, YP)
        moved[line, :] = (
            here
            + weights[0, line, :] * (west - here)
            + weights[1, line, :] * (east - here)
            + weights[2, line, :] * (south - here)
            + weights[3, line, :] * (north - here)
        )
        return carry

    group = 6 * YP

    def react(c, carry):
        at = pl.multiple_of(c * group, 8)
        lines = pl.ds(at, group)
        part = moved[lines, :]
        reacted = jnp.dot(part, coupling_ref[...], precision=HIGHEST, preferred_element_type=jnp.float32)
        state[pl.ds(at + YP, group), :] = part + weights[4, lines, :] * reacted
        return carry

    for _ in range(STEPS):
        lax.fori_loop(0, NXE, transport_line, 0, unroll=2)
        lax.fori_loop(0, NXE // 6, react, 0)

    def gradient(x):
        at = pl.multiple_of((x + 4) * YP + Y0, 8)
        return state[pl.ds(at, YO), :].astype(jnp.bfloat16).astype(jnp.float32)

    def row(table, x):
        return lon_ref[table, pl.ds(x, 1), :]

    def ahead(x, held):
        held = row(0, x) * held + row(1, x) * gradient(x)
        local_ref[x] = held
        return held

    zero = jnp.zeros((YO, S), jnp.float32)
    edge_ref[0] = lax.fori_loop(0, NX, ahead, zero, unroll=2)

    def behind(i, held):
        x = NX - 1 - i
        quarter = row(1, x)
        local_ref[x] = quarter * (local_ref[x] + held)
        return row(0, x) * (quarter * gradient(x) + held)

    edge_ref[1] = lax.fori_loop(0, NX, behind, zero, unroll=2)


def carries(received, coef_ref):
    ahead = jnp.zeros(received[0].shape[1:], jnp.float32)
    behind = ahead
    for k, ref in enumerate(received):
        ahead = ahead + coef_ref[6 * k + 4 : 6 * k + 5, :] * ref[0]
        behind = behind + coef_ref[6 * k + 5 : 6 * k + 6, :] * ref[1]
    return ahead, behind


def lat_kernel(local_ref, r0, r1, r2, r3, coef_ref, lon_ref, lat_ref, out_ref, edge_ref, plane, held_ref):
    ahead_in, behind_in = carries((r0, r1, r2, r3), coef_ref)

    def along_lon(x, carry):
        at = pl.multiple_of(x * YO, 8)
        plane[pl.ds(at, YO), :] = (
            local_ref[x]
            + lon_ref[2, pl.ds(x, 1), :] * ahead_in
            + lon_ref[3, pl.ds(x, 1), :] * behind_in
        )
        return carry

    lax.fori_loop(0, NX, along_lon, 0, unroll=2)
    held = jnp.zeros((NX, S), jnp.float32)
    for y in range(NY):
        held = lat_ref[0, y : y + 1, :] * held + lat_ref[1, y : y + 1, :] * plane[pl.ds(y, NX, stride=YO), :]
        held_ref[y] = held
    edge_ref[0, :NX, :] = held
    edge_ref[0, NX:, :] = jnp.zeros((YO - NX, S), jnp.float32)
    held = jnp.zeros((NX, S), jnp.float32)
    for y in range(NY - 1, -1, -1):
        quarter = lat_ref[1, y : y + 1, :]
        value = plane[pl.ds(y, NX, stride=YO), :]
        out_ref[pl.ds(y, NX, stride=YO), :] = quarter * (held_ref[y] + held)
        held = lat_ref[0, y : y + 1, :] * (quarter * value + held)
    edge_ref[1, :NX, :] = held
    edge_ref[1, NX:, :] = jnp.zeros((YO - NX, S), jnp.float32)


def finish_kernel(local_ref, r0, r1, r2, coef_ref, lat_ref, out_ref, carry_ref):
    carry_ref[0], carry_ref[1] = carries((r0, r1, r2), coef_ref)
    ahead, behind = lat_ref[2][:NY], lat_ref[3][:NY]

    def line(x, carry):
        at = pl.multiple_of(x * YO, 8)
        value = (
            local_ref[pl.ds(at, NY), :]
            + ahead * carry_ref[0, pl.ds(x, 1), :]
            + behind * carry_ref[1, pl.ds(x, 1), :]
        )
        out_ref[x] = value.astype(jnp.bfloat16)
        return carry

    lax.fori_loop(0, NX, line, 0, unroll=2)


def call(kernel, outs, scratch=()):
    return pl.pallas_call(
        kernel,
        out_shape=outs,
        scratch_shapes=list(scratch),
        compiler_params=pltpu.CompilerParams(vmem_limit_bytes=40 * 2**20),
    )


def f32(*shape):
    return jax.ShapeDtypeStruct(shape, jnp.float32)


def swap(x, axis, mask):
    return lax.ppermute(x, axis, [(i, i ^ mask) for i in range(lax.axis_size(axis))])


def three_parts(x):
    high = lax.reduce_precision(x, 8, 7)
    rest = x - high
    middle = lax.reduce_precision(rest, 8, 7)
    low = rest - middle
    return jnp.concatenate([high, middle, low], 0).astype(jnp.bfloat16)


def join_parts(parts):
    third = parts.shape[0] // 3
    parts = parts.astype(jnp.float32)
    return (parts[:third] + parts[third : 2 * third]) + parts[2 * third :]


def pack(cells, coefs):
    wide = jnp.pad(coefs, ((0, 0), (0, S - coefs.shape[1])))
    return jnp.concatenate([cells.reshape(-1, S), three_parts(wide)], 0)


def unpack(rows, n, m, w):
    return rows[: n * m].reshape(n, m, S), join_parts(rows[n * m :])[:, :w]


def exchange_rates(lon_rate, lat_rate):
    lon = lon_rate[0].reshape(TI, 1, NX)
    lat = lat_rate[0].reshape(1, TJ, NY)
    shape = (TI, TJ)
    columns = [
        jnp.broadcast_to(lon, shape + (NX,)),
        jnp.zeros(shape + (YO - NX,), jnp.float32),
        jnp.broadcast_to(lat, shape + (NY,)),
        jnp.zeros(shape + (YO - NY,), jnp.float32),
        jnp.broadcast_to(jnp.sum(lon, 2).reshape(1, 1, TI), shape + (TI,)),
        jnp.broadcast_to(jnp.sum(lat, 2).reshape(1, 1, TJ), shape + (TJ,)),
        jnp.zeros(shape + (S - 2 * YO - TI - TJ,), jnp.float32),
    ]
    sent = jnp.concatenate(columns, 2).reshape(TI * TJ, S)
    return lax.all_to_all(sent, "tile", split_axis=0, concat_axis=0, tiled=True)


def on_device(
    forcing, transport, reactivity, jacobian, pattern, lon_rate, lat_rate, vertical, step_scale, control
):
    cells = forcing[0, 0]
    tile = lax.axis_index("tile")
    tiles = TI * TJ
    rates = exchange_rates(lon_rate, lat_rate)

    coefs = jnp.concatenate([transport[:, 0, 0], reactivity[0, 0][None]], 0)
    northward = pack(
        jnp.swapaxes(cells[:, NY - 3 :], 0, 1),
        jnp.swapaxes(coefs[:, :, NY - 2 :], 1, 2).reshape(2 * FLD, NX),
    )
    southward = pack(
        jnp.swapaxes(cells[:, :3], 0, 1), jnp.swapaxes(coefs[:, :, :2], 1, 2).reshape(2 * FLD, NX)
    )
    steps_up = [(i, i + 1) for i in range(tiles) if i % TJ < TJ - 1]
    from_south = lax.ppermute(northward, "tile", steps_up)
    from_north = lax.ppermute(southward, "tile", [(b, a) for a, b in steps_up])
    south, south_coefs = unpack(from_south, 3, NX, NX)
    north, north_coefs = unpack(from_north, 3, NX, NX)
    south_coefs = jnp.swapaxes(south_coefs.reshape(FLD, 2, NX), 1, 2)
    north_coefs = jnp.swapaxes(north_coefs.reshape(FLD, 2, NX), 1, 2)
    tall = jnp.concatenate([south_coefs, coefs, north_coefs], 2)

    def side(lines):
        return jnp.concatenate(
            [jnp.swapaxes(south[1:, lines], 0, 1), cells[lines], jnp.swapaxes(north[:2, lines], 0, 1)], 1
        )

    eastward = pack(side(slice(NX - 3, NX)), tall[:, NX - 2 :].reshape(2 * FLD, NY + 4))
    westward = pack(side(slice(0, 3)), tall[:, :2].reshape(2 * FLD, NY + 4))
    from_west = lax.ppermute(eastward, "tile", [(i, (i + TJ) % tiles) for i in range(tiles)])
    from_east = lax.ppermute(westward, "tile", [((i + TJ) % tiles, i) for i in range(tiles)])
    west, west_coefs = unpack(from_west, 3, NY + 4, NY + 4)
    east, east_coefs = unpack(from_east, 3, NY + 4, NY + 4)
    planes = jnp.concatenate(
        [west_coefs.reshape(FLD, 2, NY + 4), tall, east_coefs.reshape(FLD, 2, NY + 4)], 1
    )
    planes = jnp.pad(planes, ((0, 0), (1, YP - NX - 5), (Y0 - 2, S - NY - 2 - Y0)))

    lon_masks, lon_gates = scan_tables(TI)
    lat_masks, lat_gates = scan_tables(TJ)
    at_lon, at_lat = tile // TJ, tile % TJ

    def pick(table, at):
        return lax.dynamic_index_in_dim(jnp.asarray(table), at, 0, keepdims=False)

    lon, lat, lon_coef, lat_coef = call(
        tables_kernel, (f32(4, YO, S), f32(4, YO, S), f32(6 * 4, S), f32(6 * 3, S))
    )(rates, pick(lon_masks, at_lon), pick(lat_masks, at_lat), pick(lon_gates, at_lon), pick(lat_gates, at_lat))

    groups = pattern.shape[0]
    width = S // groups
    blockmask = jnp.broadcast_to(
        pattern.astype(jnp.float32)[:, None, :, None], (groups, width, groups, width)
    ).reshape(S, S)
    coupling = jacobian[0] * blockmask

    local, edge = call(
        steps_kernel,
        (f32(NX, YO, S), f32(2, YO, S)),
        (
            pltpu.VMEM(((NXE + 2) * YP, S), jnp.float32),
            pltpu.VMEM((NXE * YP, S), jnp.float32),
            pltpu.VMEM((FLD, NXE * YP, S), jnp.float32),
        ),
    )(cells, south, north, west, east, planes, coupling, lon)

    def rounds(edge, coef, bits):
        received = []
        for k, mask in enumerate(bits):
            other = swap(edge, "tile", mask)
            received.append(other)
            if k + 1 < len(bits):
                mine = coef[jnp.array([6 * k, 6 * k + 2])][:, None]
                theirs = coef[jnp.array([6 * k + 1, 6 * k + 3])][:, None]
                edge = mine * edge + theirs * other
        return received

    local, edge = call(
        lat_kernel,
        (f32(NX * YO, S), f32(2, YO, S)),
        (pltpu.VMEM((NX * YO, S), jnp.float32), pltpu.VMEM((NY, NX, S), jnp.float32)),
    )(local, *rounds(edge, lon_coef, LON_MASKS), lon_coef, lon, lat)
    filtered = call(
        finish_kernel,
        jax.ShapeDtypeStruct((NX, NY, S), jnp.bfloat16),
        (pltpu.VMEM((2, YO, S), jnp.float32),),
    )(local, *rounds(edge, lat_coef, LAT_MASKS), lat_coef, lat)

    levels = [filtered, swap(filtered, "lev", 1), swap(filtered, "lev", 2)]
    levels.append(swap(levels[2], "lev", 1))
    level_here = lax.axis_index("lev")
    mixing = lax.dynamic_index_in_dim(vertical, level_here, 1, keepdims=False).T
    increment = jnp.zeros((NX, NY, S), jnp.float32)
    for mask, plane in enumerate(levels):
        factor = lax.dynamic_index_in_dim(mixing, level_here ^ mask, 0, keepdims=False)
        increment = increment + factor * plane.astype(jnp.float32)
    updated = control[0, 0].astype(jnp.float32) - step_scale * increment
    return updated.astype(jnp.bfloat16)[None, None]


def solution(mesh):
    in_specs = (
        P("lev", "tile", None, None, None),
        P(None, "lev", "tile", None, None),
        P("lev", "tile", None, None),
        P("lev", None, None),
        P(),
        P("tile", None),
        P("tile", None),
        P(),
        P(),
        P("lev", "tile", None, None, None),
    )
    out_specs = P("lev", "tile", None, None, None)
    return jax.shard_map(
        on_device, mesh=mesh, in_specs=in_specs, out_specs=out_specs, check_vma=False
    )
```

```python
import jax
import jax.numpy as jnp
from jax import lax
from jax.experimental import pallas as pl
from jax.experimental.pallas import tpu as pltpu
from jax.sharding import PartitionSpec as P

TJ = 8
TI = 16
STEPS = 3
NX = 36
NY = 36
S = 128
YP = 48
Y0 = 8
YO = 40
FLD = 5
HIGHEST = lax.Precision.HIGHEST
VMEM = pl.BlockSpec(memory_space=pltpu.VMEM)
LON_MASKS = (8, 16, 32, 64)
LAT_MASKS = (1, 2, 4)


def round_factors(me, sums, bits):
    tiles, rows = sums.shape[0], 6 * bits
    row = lax.broadcasted_iota(jnp.int32, (rows, tiles), 0)
    tile = lax.broadcasted_iota(jnp.int32, (rows, tiles), 1)
    level = jnp.zeros_like(row)
    for k in range(1, bits):
        level = level + (row >= 6 * k).astype(jnp.int32)
    kind = row - 6 * level
    here = jnp.full_like(row, me)
    block = lax.shift_right_logical(here, level)
    of_tile = lax.shift_right_logical(tile, level)
    upper = (block & 1) == 1
    own = of_tile == block
    other = of_tile == block + 1 - 2 * (block & 1)
    used = (
        ((kind == 0) & ~upper & other)
        | ((kind == 1) & upper & other)
        | ((kind == 2) & upper & own)
        | ((kind == 3) & ~upper & own)
        | ((kind == 4) & own & (tile < here))
        | ((kind == 5) & own & (tile > here))
    )
    total = jnp.dot(used.astype(jnp.float32), sums, precision=HIGHEST, preferred_element_type=jnp.float32)
    off = ((kind == 4) & ~upper) | ((kind == 5) & upper)
    gate = 1.0 - off.astype(jnp.float32)[:, :1]
    return gate * jnp.exp(-total)


def put_line(state, at, value):
    state[at : at + Y0, :] = jnp.zeros((Y0, S), jnp.float32)
    state[at + YP - 8 : at + YP, :] = jnp.zeros((8, S), jnp.float32)
    first = Y0 - (value.shape[0] - NY) // 2
    state[at + first : at + first + value.shape[0], :] = value


def put_rims(state, south_ref, north_ref, base, lines, skip):
    for j in range(3):
        for ref, row in ((south_ref, Y0 - 3 + j), (north_ref, Y0 + NY + j)):
            rim = ref[j][skip : skip + lines].astype(jnp.float32)
            state[pl.ds(base + row, lines, stride=YP), :] = rim


def put_weights(weights, planes_ref, first, lines):
    for f in range(FLD):
        column = planes_ref[f].T
        for x in range(lines):
            spread = jnp.broadcast_to(column[:YP, first + x : first + x + 1], (YP, S))
            weights[f, x * YP : (x + 1) * YP, :] = spread


def advance(source, weights, large, small, at, wat, lines):
    size = lines * YP
    here = source[at : at + size, :]
    west = source[at - YP : at - YP + size, :]
    east = source[at + YP : at + YP + size, :]
    south = pltpu.roll(here, 1, 0)
    north = pltpu.roll(here, size - 1, 0)
    moved = (
        here
        + weights[0, wat : wat + size, :] * (west - here)
        + weights[1, wat : wat + size, :] * (east - here)
        + weights[2, wat : wat + size, :] * (south - here)
        + weights[3, wat : wat + size, :] * (north - here)
    )
    m1, m2, m3 = split(moved)
    top = jnp.dot(jnp.concatenate([m1, m2], 1), large, preferred_element_type=jnp.float32)
    low = jnp.dot(jnp.concatenate([m3, m1], 1), small, preferred_element_type=jnp.float32)
    reacted = top[:, :S] + (top[:, S:] + low)
    return moved + weights[4, wat : wat + size, :] * reacted


def round_gradient(result, line):
    part = result[line * YP + Y0 : line * YP + Y0 + YO]
    return part.astype(jnp.bfloat16).astype(jnp.float32)


def inner_kernel(
    forcing_ref, south_ref, north_ref, planes_ref, pattern_ref, jacobian_ref,
    gradient_ref, between_ref, large_ref, small_ref,
    even, odd, weights, pattern_copy, jacobian_copy, arrived,
):
    fetches = [
        pltpu.make_async_copy(pattern_ref, pattern_copy, arrived.at[0]),
        pltpu.make_async_copy(jacobian_ref, jacobian_copy, arrived.at[1]),
    ]
    for fetch in fetches:
        fetch.start()
    for x in range(NX):
        put_line(even, x * YP, forcing_ref[x].astype(jnp.float32))
    put_rims(even, south_ref, north_ref, 0, NX, 0)
    put_weights(weights, planes_ref, 0, NX)

    for fetch in fetches:
        fetch.wait()
    blocks = pattern_copy.shape[0]
    spread = (
        lax.broadcasted_iota(jnp.int32, (blocks, S), 0)
        == lax.broadcasted_iota(jnp.int32, (blocks, S), 1) // (S // blocks)
    ).astype(jnp.float32)
    wide = jnp.dot(pattern_copy[...].astype(jnp.float32), spread, preferred_element_type=jnp.float32)
    mask = lax.dot_general(spread, wide, (((0,), (0,)), ((), ())), preferred_element_type=jnp.float32)
    w1, w2, w3 = split(jacobian_copy[...] * mask)
    both = jnp.concatenate([w1, w2], 1)
    large = jnp.concatenate([both, both], 0)
    small = jnp.concatenate([w1, w3], 0)
    large_ref[...] = large
    small_ref[...] = small

    source, target = even, odd
    for step in range(STEPS):
        first, last = 1 + step, NX - 1 - step
        groups = [(x, min(4, last - x)) for x in range(first, last, 4)]
        for x, lines in groups:
            result = advance(source, weights, large, small, x * YP, x * YP, lines)
            if step == STEPS - 1:
                for i in range(lines):
                    gradient_ref[x - 3 + i] = round_gradient(result, i)
            else:
                target[x * YP : (x + lines) * YP, :] = result
        if step < STEPS - 1:
            for i, x in enumerate((1 + step, 2 + step, NX - 3 - step, NX - 2 - step)):
                between_ref[4 * step + i] = target[x * YP : (x + 1) * YP, :]
        source, target = target, source


def outer_kernel(
    forcing_ref, south_ref, north_ref, west_ref, east_ref, planes_ref, between_ref, large_ref, small_ref,
    gradient_ref, zero, one, two, weights,
):
    large, small = large_ref[...], small_ref[...]
    slots = 6
    for side in range(2):
        base = side * slots * YP
        halo = (west_ref, east_ref)[side]
        for i in range(3):
            slot = i if side == 0 else i + 2
            put_line(zero, base + slot * YP, halo[i].astype(jnp.float32))
        first = 0 if side == 0 else NX - 2
        slot = 3 if side == 0 else 0
        for i in range(2):
            put_line(zero, base + (slot + i) * YP, forcing_ref[first + i].astype(jnp.float32))
        put_rims(zero, south_ref, north_ref, base + slot * YP, 2, first)
        put_weights(weights.at[side], planes_ref, 1 if side == 0 else NX, 5)

    def at(side, slot):
        return (side * slots + slot) * YP

    for side in range(2):
        done = advance(zero, weights.at[side], large, small, at(side, 1), 0 if side == 0 else 2 * YP, 3)
        for i in range(3):
            slot = i if side == 0 else i + 2
            one[at(side, slot) : at(side, slot + 1), :] = done[i * YP : (i + 1) * YP]
        for i in range(2):
            slot = i + 3 if side == 0 else i
            one[at(side, slot) : at(side, slot + 1), :] = between_ref[2 * side + i]
    for side in range(2):
        done = advance(one, weights.at[side], large, small, at(side, 1), YP, 3)
        for i in range(3):
            slot = i if side == 0 else i + 2
            two[at(side, slot) : at(side, slot + 1), :] = done[i * YP : (i + 1) * YP]
        for i in range(2):
            slot = i + 3 if side == 0 else i
            two[at(side, slot) : at(side, slot + 1), :] = between_ref[4 + 2 * side + i]
    for side in range(2):
        done = advance(two, weights.at[side], large, small, at(side, 1), 2 * YP if side == 0 else 0, 3)
        for i in range(3):
            gradient_ref[3 * side + i] = round_gradient(done, i)


def split(x):
    high = x.astype(jnp.bfloat16)
    rest = x - high.astype(jnp.float32)
    middle = rest.astype(jnp.bfloat16)
    return high, middle, (rest - middle.astype(jnp.float32)).astype(jnp.bfloat16)


def lon_kernel(
    me_ref, inner_ref, outer_ref, rate_ref, local_ref, edge_ref, lon_ref, lat_ref, lonc_ref, latc_ref
):
    fields = rate_ref[...].T
    row = lax.broadcasted_iota(jnp.int32, (YO, YO), 0)
    col = lax.broadcasted_iota(jnp.int32, (YO, YO), 1)
    upto = (col <= row).astype(jnp.float32)
    after = (col > row).astype(jnp.float32)
    for first, out in ((0, lon_ref), (YO, lat_ref)):
        rates = fields[first : first + YO]
        quarter = jnp.sqrt(jnp.sqrt(rates))
        before = jnp.dot(upto, rates, precision=HIGHEST, preferred_element_type=jnp.float32)
        beyond = jnp.dot(after, rates, precision=HIGHEST, preferred_element_type=jnp.float32)
        out[0] = jnp.exp(-rates)
        out[1] = quarter
        out[2] = quarter * jnp.exp(-before)
        out[3] = quarter * jnp.exp(-beyond)
    lonc_ref[...] = round_factors(me_ref[0] // TJ, fields[2 * YO : 2 * YO + TI], len(LON_MASKS))
    latc_ref[...] = round_factors(me_ref[0] % TJ, fields[2 * YO + TI : 2 * YO + TI + TJ], len(LAT_MASKS))

    def gradient(x):
        if x < 3:
            return outer_ref[x]
        return inner_ref[x - 3] if x < NX - 3 else outer_ref[x - NX + 6]

    held = jnp.zeros((YO, S), jnp.float32)
    for x in range(NX):
        held = lon_ref[0, x : x + 1, :] * held + lon_ref[1, x : x + 1, :] * gradient(x)
        local_ref[x] = held
    edge_ref[0] = held
    held = jnp.zeros((YO, S), jnp.float32)
    for x in range(NX - 1, -1, -1):
        quarter = lon_ref[1, x : x + 1, :]
        local_ref[x] = quarter * (local_ref[x] + held)
        held = lon_ref[0, x : x + 1, :] * (quarter * gradient(x) + held)
    edge_ref[1] = held


def carries(received, coef_ref):
    ahead = jnp.zeros(received[0].shape[1:], jnp.float32)
    behind = ahead
    for k, ref in enumerate(received):
        ahead = ahead + coef_ref[6 * k + 4 : 6 * k + 5, :] * ref[0]
        behind = behind + coef_ref[6 * k + 5 : 6 * k + 6, :] * ref[1]
    return ahead, behind


def lat_kernel(local_ref, r0, r1, r2, r3, coef_ref, lon_ref, lat_ref, out_ref, edge_ref, plane, held_ref):
    ahead_in, behind_in = carries((r0, r1, r2, r3), coef_ref)

    def along_lon(x, carry):
        at = pl.multiple_of(x * YO, 8)
        plane[pl.ds(at, YO), :] = (
            local_ref[x]
            + lon_ref[2, pl.ds(x, 1), :] * ahead_in
            + lon_ref[3, pl.ds(x, 1), :] * behind_in
        )
        return carry

    lax.fori_loop(0, NX, along_lon, 0, unroll=2)
    held = jnp.zeros((NX, S), jnp.float32)
    for y in range(NY):
        held = lat_ref[0, y : y + 1, :] * held + lat_ref[1, y : y + 1, :] * plane[pl.ds(y, NX, stride=YO), :]
        held_ref[y] = held
    edge_ref[0, :NX, :] = held
    edge_ref[0, NX:, :] = jnp.zeros((YO - NX, S), jnp.float32)
    held = jnp.zeros((NX, S), jnp.float32)
    for y in range(NY - 1, -1, -1):
        quarter = lat_ref[1, y : y + 1, :]
        value = plane[pl.ds(y, NX, stride=YO), :]
        out_ref[pl.ds(y, NX, stride=YO), :] = quarter * (held_ref[y] + held)
        held = lat_ref[0, y : y + 1, :] * (quarter * value + held)
    edge_ref[1, :NX, :] = held
    edge_ref[1, NX:, :] = jnp.zeros((YO - NX, S), jnp.float32)


def finish_kernel(local_ref, r0, r1, r2, coef_ref, lat_ref, out_ref, carry_ref):
    carry_ref[0], carry_ref[1] = carries((r0, r1, r2), coef_ref)
    ahead, behind = lat_ref[2][:NY], lat_ref[3][:NY]

    def line(x, carry):
        at = pl.multiple_of(x * YO, 8)
        value = (
            local_ref[pl.ds(at, NY), :]
            + ahead * carry_ref[0, pl.ds(x, 1), :]
            + behind * carry_ref[1, pl.ds(x, 1), :]
        )
        out_ref[x] = value.astype(jnp.bfloat16)
        return carry

    lax.fori_loop(0, NX, line, 0, unroll=2)


def call(kernel, outs, scratch=(), specs=None):
    def run(*operands):
        return built(len(operands))(*operands)

    def built(count):
        return pl.pallas_call(
        kernel,
        out_shape=outs,
        in_specs=specs or [VMEM] * count,
        scratch_shapes=list(scratch),
        compiler_params=pltpu.CompilerParams(vmem_limit_bytes=40 * 2**20),
    )

    return run


def f32(*shape):
    return jax.ShapeDtypeStruct(shape, jnp.float32)


def swap(x, axis, mask):
    return lax.ppermute(x, axis, [(i, i ^ mask) for i in range(lax.axis_size(axis))])


def three_parts(x):
    high = lax.reduce_precision(x, 8, 7)
    rest = x - high
    middle = lax.reduce_precision(rest, 8, 7)
    low = rest - middle
    return jnp.concatenate([high, middle, low], 0).astype(jnp.bfloat16)


def join_parts(parts):
    third = parts.shape[0] // 3
    parts = parts.astype(jnp.float32)
    return (parts[:third] + parts[third : 2 * third]) + parts[2 * third :]


def widen(coefs, before, after):
    return jnp.pad(coefs, ((0, 0), (before, after), (Y0 - 2, S - NY - 2 - Y0)))


def pack(cells, coefs):
    wide = jnp.pad(coefs, ((0, 0), (0, S - coefs.shape[1])))
    return jnp.concatenate([cells.reshape(-1, S), three_parts(wide)], 0)


def unpack(rows, n, m, w):
    return rows[: n * m].reshape(n, m, S), join_parts(rows[n * m :])[:, :w]


def rate_rows(lon_rate, lat_rate):
    lon = lon_rate[0].reshape(TI, 1, NX)
    lat = lat_rate[0].reshape(1, TJ, NY)
    shape = (TI, TJ)
    columns = [
        jnp.broadcast_to(lon, shape + (NX,)),
        jnp.zeros(shape + (YO - NX,), jnp.float32),
        jnp.broadcast_to(lat, shape + (NY,)),
        jnp.zeros(shape + (YO - NY,), jnp.float32),
        jnp.broadcast_to(jnp.sum(lon, 2).reshape(1, 1, TI), shape + (TI,)),
        jnp.broadcast_to(jnp.sum(lat, 2).reshape(1, 1, TJ), shape + (TJ,)),
        jnp.zeros(shape + (S - 2 * YO - TI - TJ,), jnp.float32),
    ]
    return jnp.concatenate(columns, 2).reshape(TI * TJ, S)


def one_device(
    forcing, transport, reactivity, jacobian, pattern, lon_rate, lat_rate, vertical, step_scale, control
):
    cells = forcing[0, 0]
    tile = lax.axis_index("tile")
    tiles = TI * TJ

    coefs = jnp.concatenate([transport[:, 0, 0], reactivity[0, 0][None]], 0)
    northward = pack(
        jnp.swapaxes(cells[:, NY - 3 :], 0, 1),
        jnp.swapaxes(coefs[:, :, NY - 2 :], 1, 2).reshape(2 * FLD, NX),
    )
    southward = pack(
        jnp.swapaxes(cells[:, :3], 0, 1), jnp.swapaxes(coefs[:, :, :2], 1, 2).reshape(2 * FLD, NX)
    )
    steps_up = [(i, i + 1) for i in range(tiles) if i % TJ < TJ - 1]
    from_south = lax.ppermute(northward, "tile", steps_up)
    from_north = lax.ppermute(southward, "tile", [(b, a) for a, b in steps_up])
    south, south_coefs = unpack(from_south, 3, NX, NX)
    north, north_coefs = unpack(from_north, 3, NX, NX)
    south_coefs, north_coefs, sent = lax.optimization_barrier(
        (south_coefs, north_coefs, rate_rows(lon_rate, lat_rate))
    )
    rates = lax.all_to_all(sent, "tile", split_axis=0, concat_axis=0, tiled=True)
    south_coefs = jnp.swapaxes(south_coefs.reshape(FLD, 2, NX), 1, 2)
    north_coefs = jnp.swapaxes(north_coefs.reshape(FLD, 2, NX), 1, 2)
    tall = jnp.concatenate([south_coefs, coefs, north_coefs], 2)

    def side(lines):
        return jnp.concatenate(
            [jnp.swapaxes(south[1:, lines], 0, 1), cells[lines], jnp.swapaxes(north[:2, lines], 0, 1)], 1
        )

    eastward = pack(side(slice(NX - 3, NX)), tall[:, NX - 2 :].reshape(2 * FLD, NY + 4))
    westward = pack(side(slice(0, 3)), tall[:, :2].reshape(2 * FLD, NY + 4))
    from_west = lax.ppermute(eastward, "tile", [(i, (i + TJ) % tiles) for i in range(tiles)])
    from_east = lax.ppermute(westward, "tile", [((i + TJ) % tiles, i) for i in range(tiles)])
    inner, between, large, small = call(
        inner_kernel,
        (
            f32(NX - 6, YO, S),
            f32(8, YP, S),
            jax.ShapeDtypeStruct((2 * S, 2 * S), jnp.bfloat16),
            jax.ShapeDtypeStruct((2 * S, S), jnp.bfloat16),
        ),
        (
            pltpu.VMEM((NX * YP, S), jnp.float32),
            pltpu.VMEM((NX * YP, S), jnp.float32),
            pltpu.VMEM((FLD, NX * YP, S), jnp.float32),
            pltpu.VMEM(pattern.shape, pattern.dtype),
            pltpu.VMEM((S, S), jnp.float32),
            pltpu.SemaphoreType.DMA((2,)),
        ),
        specs=[VMEM] * 4 + [pl.BlockSpec(memory_space=pl.ANY)] * 2,
    )(cells, south, north, widen(tall, 0, YP - NX), pattern, jacobian[0])
    west, west_coefs = unpack(from_west, 3, NY + 4, NY + 4)
    east, east_coefs = unpack(from_east, 3, NY + 4, NY + 4)
    planes = jnp.concatenate(
        [west_coefs.reshape(FLD, 2, NY + 4), tall, east_coefs.reshape(FLD, 2, NY + 4)], 1
    )
    planes = widen(planes, 1, YP - NX - 5)

    outer = call(
        outer_kernel,
        f32(6, YO, S),
        tuple(pltpu.VMEM((12 * YP, S), jnp.float32) for _ in range(3))
        + (pltpu.VMEM((2, FLD, 5 * YP, S), jnp.float32),),
    )(cells, south, north, west, east, planes, between, large, small)
    local, edge, lon, lat, lon_coef, lat_coef = call(
        lon_kernel,
        (f32(NX, YO, S), f32(2, YO, S), f32(4, YO, S), f32(4, YO, S), f32(6 * 4, S), f32(6 * 3, S)),
        specs=[pl.BlockSpec(memory_space=pltpu.SMEM), VMEM, VMEM, VMEM],
    )(tile.reshape(1), inner, outer, rates)

    def rounds(edge, coef, bits):
        received = []
        for k, mask in enumerate(bits):
            other = swap(edge, "tile", mask)
            received.append(other)
            if k + 1 < len(bits):
                mine = coef[6 * k : 6 * k + 2][:, None]
                theirs = coef[6 * k + 2 : 6 * k + 4][:, None]
                edge = mine * edge + theirs * other
        return received

    level_here = lax.axis_index("lev")
    mixing = lax.dynamic_index_in_dim(vertical, level_here, 1, keepdims=False).T
    factors = [
        step_scale * lax.dynamic_index_in_dim(mixing, level_here ^ mask, 0, keepdims=False)
        for mask in range(4)
    ]
    received = rounds(edge, lon_coef, LON_MASKS)
    received[0], *factors = lax.optimization_barrier((received[0], *factors))
    local, edge = call(
        lat_kernel,
        (f32(NX * YO, S), f32(2, YO, S)),
        (pltpu.VMEM((NX * YO, S), jnp.float32), pltpu.VMEM((NY, NX, S), jnp.float32)),
    )(local, *received, lon_coef, lon, lat)
    filtered = call(
        finish_kernel,
        jax.ShapeDtypeStruct((NX, NY, S), jnp.bfloat16),
        (pltpu.VMEM((2, YO, S), jnp.float32),),
    )(local, *rounds(edge, lat_coef, LAT_MASKS), lat_coef, lat)

    levels = [filtered, swap(filtered, "lev", 1), swap(filtered, "lev", 2)]
    levels.append(swap(levels[2], "lev", 1))
    increment = jnp.zeros((NX, NY, S), jnp.float32)
    for factor, plane in zip(factors, levels):
        increment = increment + factor * plane.astype(jnp.float32)
    updated = control[0, 0].astype(jnp.float32) - increment
    return updated.astype(jnp.bfloat16)[None, None]


def solution(mesh):
    in_specs = (
        P("lev", "tile", None, None, None),
        P(None, "lev", "tile", None, None),
        P("lev", "tile", None, None),
        P("lev", None, None),
        P(),
        P("tile", None),
        P("tile", None),
        P(),
        P(),
        P("lev", "tile", None, None, None),
    )
    out_specs = P("lev", "tile", None, None, None)
    return jax.shard_map(one_device, mesh=mesh, in_specs=in_specs, out_specs=out_specs, check_vma=False)
```

```python
import jax
import jax.numpy as jnp
from jax import lax
from jax.experimental import pallas as pl
from jax.experimental.pallas import tpu as pltpu
from jax.sharding import PartitionSpec as P

TJ = 8
TI = 16
STEPS = 3
NX = 36
NY = 36
S = 128
YP = 48
Y0 = 8
YO = 40
FLD = 5
HIGHEST = lax.Precision.HIGHEST
VMEM = pl.BlockSpec(memory_space=pltpu.VMEM)
LON_MASKS = (8, 16, 32, 64)
LAT_MASKS = (1, 2, 4)


def round_factors(me, sums, bits):
    tiles, rows = sums.shape[0], 6 * bits
    row = lax.broadcasted_iota(jnp.int32, (rows, tiles), 0)
    tile = lax.broadcasted_iota(jnp.int32, (rows, tiles), 1)
    level = jnp.zeros_like(row)
    for k in range(1, bits):
        level = level + (row >= 6 * k).astype(jnp.int32)
    kind = row - 6 * level
    here = jnp.full_like(row, me)
    block = lax.shift_right_logical(here, level)
    of_tile = lax.shift_right_logical(tile, level)
    upper = (block & 1) == 1
    own = of_tile == block
    other = of_tile == block + 1 - 2 * (block & 1)
    used = (
        ((kind == 0) & ~upper & other)
        | ((kind == 1) & upper & other)
        | ((kind == 2) & upper & own)
        | ((kind == 3) & ~upper & own)
        | ((kind == 4) & own & (tile < here))
        | ((kind == 5) & own & (tile > here))
    )
    total = jnp.dot(used.astype(jnp.float32), sums, precision=HIGHEST, preferred_element_type=jnp.float32)
    off = ((kind == 4) & ~upper) | ((kind == 5) & upper)
    gate = 1.0 - off.astype(jnp.float32)[:, :1]
    return gate * jnp.exp(-total)


def put_line(state, at, value):
    state[at : at + Y0, :] = jnp.zeros((Y0, S), jnp.float32)
    state[at + YP - 8 : at + YP, :] = jnp.zeros((8, S), jnp.float32)
    first = Y0 - (value.shape[0] - NY) // 2
    state[at + first : at + first + value.shape[0], :] = value


def put_rims(state, south_ref, north_ref, base, lines, skip):
    for j in range(3):
        for ref, row in ((south_ref, Y0 - 3 + j), (north_ref, Y0 + NY + j)):
            rim = ref[j][skip : skip + lines].astype(jnp.float32)
            state[pl.ds(base + row, lines, stride=YP), :] = rim


def put_weights(weights, planes_ref, first, lines):
    for f in range(FLD):
        column = planes_ref[f].T
        for x in range(lines):
            spread = jnp.broadcast_to(column[:YP, first + x : first + x + 1], (YP, S))
            weights[f, x * YP : (x + 1) * YP, :] = spread


def advance(source, weights, large, small, at, wat, lines):
    size = lines * YP
    here = source[at : at + size, :]
    west = source[at - YP : at - YP + size, :]
    east = source[at + YP : at + YP + size, :]
    south = pltpu.roll(here, 1, 0)
    north = pltpu.roll(here, size - 1, 0)
    moved = (
        here
        + weights[0, wat : wat + size, :] * (west - here)
        + weights[1, wat : wat + size, :] * (east - here)
        + weights[2, wat : wat + size, :] * (south - here)
        + weights[3, wat : wat + size, :] * (north - here)
    )
    m1, m2, m3 = split(moved)
    top = jnp.dot(jnp.concatenate([m1, m2], 1), large, preferred_element_type=jnp.float32)
    low = jnp.dot(jnp.concatenate([m3, m1], 1), small, preferred_element_type=jnp.float32)
    reacted = top[:, :S] + (top[:, S:] + low)
    return moved + weights[4, wat : wat + size, :] * reacted


def round_gradient(result, line):
    part = result[line * YP + Y0 : line * YP + Y0 + YO]
    return part.astype(jnp.bfloat16).astype(jnp.float32)


def inner_kernel(
    forcing_ref, south_ref, north_ref, planes_ref, pattern_ref, jacobian_ref,
    gradient_ref, between_ref, large_ref, small_ref,
    even, odd, weights, pattern_copy, jacobian_copy, arrived,
):
    fetches = [
        pltpu.make_async_copy(pattern_ref, pattern_copy, arrived.at[0]),
        pltpu.make_async_copy(jacobian_ref, jacobian_copy, arrived.at[1]),
    ]
    for fetch in fetches:
        fetch.start()
    for x in range(NX):
        put_line(even, x * YP, forcing_ref[x].astype(jnp.float32))
    put_rims(even, south_ref, north_ref, 0, NX, 0)
    put_weights(weights, planes_ref, 0, NX)

    for fetch in fetches:
        fetch.wait()
    blocks = pattern_copy.shape[0]
    spread = (
        lax.broadcasted_iota(jnp.int32, (blocks, S), 0)
        == lax.broadcasted_iota(jnp.int32, (blocks, S), 1) // (S // blocks)
    ).astype(jnp.float32)
    wide = jnp.dot(pattern_copy[...].astype(jnp.float32), spread, preferred_element_type=jnp.float32)
    mask = lax.dot_general(spread, wide, (((0,), (0,)), ((), ())), preferred_element_type=jnp.float32)
    w1, w2, w3 = split(jacobian_copy[...] * mask)
    both = jnp.concatenate([w1, w2], 1)
    large = jnp.concatenate([both, both], 0)
    small = jnp.concatenate([w1, w3], 0)
    large_ref[...] = large
    small_ref[...] = small

    source, target = even, odd
    for step in range(STEPS):
        first, last = 1 + step, NX - 1 - step
        groups = [(x, min(4, last - x)) for x in range(first, last, 4)]
        for x, lines in groups:
            result = advance(source, weights, large, small, x * YP, x * YP, lines)
            if step == STEPS - 1:
                for i in range(lines):
                    gradient_ref[x - 3 + i] = round_gradient(result, i)
            else:
                target[x * YP : (x + lines) * YP, :] = result
        if step < STEPS - 1:
            for i, x in enumerate((1 + step, 2 + step, NX - 3 - step, NX - 2 - step)):
                between_ref[4 * step + i] = target[x * YP : (x + 1) * YP, :]
        source, target = target, source


def outer_kernel(
    forcing_ref, south_ref, north_ref, west_ref, east_ref, planes_ref, between_ref, large_ref, small_ref,
    gradient_ref, zero, one, two, weights,
):
    large, small = large_ref[...], small_ref[...]
    slots = 6
    for side in range(2):
        base = side * slots * YP
        halo = (west_ref, east_ref)[side]
        for i in range(3):
            slot = i if side == 0 else i + 2
            put_line(zero, base + slot * YP, halo[i].astype(jnp.float32))
        first = 0 if side == 0 else NX - 2
        slot = 3 if side == 0 else 0
        for i in range(2):
            put_line(zero, base + (slot + i) * YP, forcing_ref[first + i].astype(jnp.float32))
        put_rims(zero, south_ref, north_ref, base + slot * YP, 2, first)
        put_weights(weights.at[side], planes_ref, 1 if side == 0 else NX, 5)

    def at(side, slot):
        return (side * slots + slot) * YP

    for side in range(2):
        done = advance(zero, weights.at[side], large, small, at(side, 1), 0 if side == 0 else 2 * YP, 3)
        for i in range(3):
            slot = i if side == 0 else i + 2
            one[at(side, slot) : at(side, slot + 1), :] = done[i * YP : (i + 1) * YP]
        for i in range(2):
            slot = i + 3 if side == 0 else i
            one[at(side, slot) : at(side, slot + 1), :] = between_ref[2 * side + i]
    for side in range(2):
        done = advance(one, weights.at[side], large, small, at(side, 1), YP, 3)
        for i in range(3):
            slot = i if side == 0 else i + 2
            two[at(side, slot) : at(side, slot + 1), :] = done[i * YP : (i + 1) * YP]
        for i in range(2):
            slot = i + 3 if side == 0 else i
            two[at(side, slot) : at(side, slot + 1), :] = between_ref[4 + 2 * side + i]
    for side in range(2):
        done = advance(two, weights.at[side], large, small, at(side, 1), 2 * YP if side == 0 else 0, 3)
        for i in range(3):
            gradient_ref[3 * side + i] = round_gradient(done, i)


def split(x):
    high = x.astype(jnp.bfloat16)
    rest = x - high.astype(jnp.float32)
    middle = rest.astype(jnp.bfloat16)
    return high, middle, (rest - middle.astype(jnp.float32)).astype(jnp.bfloat16)


def lon_kernel(
    me_ref, inner_ref, outer_ref, rate_ref, local_ref, edge_ref, lon_ref, lat_ref, lonc_ref, latc_ref
):
    fields = rate_ref[...].T
    row = lax.broadcasted_iota(jnp.int32, (YO, YO), 0)
    col = lax.broadcasted_iota(jnp.int32, (YO, YO), 1)
    upto = (col <= row).astype(jnp.float32)
    after = (col > row).astype(jnp.float32)
    for first, out in ((0, lon_ref), (YO, lat_ref)):
        rates = fields[first : first + YO]
        quarter = jnp.sqrt(jnp.sqrt(rates))
        before = jnp.dot(upto, rates, precision=HIGHEST, preferred_element_type=jnp.float32)
        beyond = jnp.dot(after, rates, precision=HIGHEST, preferred_element_type=jnp.float32)
        out[0] = jnp.exp(-rates)
        out[1] = quarter
        out[2] = quarter * jnp.exp(-before)
        out[3] = quarter * jnp.exp(-beyond)
    lonc_ref[...] = round_factors(me_ref[0] // TJ, fields[2 * YO : 2 * YO + TI], len(LON_MASKS))
    latc_ref[...] = round_factors(me_ref[0] % TJ, fields[2 * YO + TI : 2 * YO + TI + TJ], len(LAT_MASKS))

    def gradient(x):
        if x < 3:
            return outer_ref[x]
        return inner_ref[x - 3] if x < NX - 3 else outer_ref[x - NX + 6]

    held = jnp.zeros((YO, S), jnp.float32)
    for x in range(NX):
        held = lon_ref[0, x : x + 1, :] * held + lon_ref[1, x : x + 1, :] * gradient(x)
        local_ref[x] = held
    edge_ref[0] = held
    held = jnp.zeros((YO, S), jnp.float32)
    for x in range(NX - 1, -1, -1):
        quarter = lon_ref[1, x : x + 1, :]
        local_ref[x] = quarter * (local_ref[x] + held)
        held = lon_ref[0, x : x + 1, :] * (quarter * gradient(x) + held)
    edge_ref[1] = held


def outer_lon_kernel(
    me_ref, forcing_ref, south_ref, north_ref, west_ref, east_ref, planes_ref, between_ref, large_ref,
    small_ref, inner_ref, rate_ref, local_ref, edge_ref, lon_ref, lat_ref, lonc_ref, latc_ref,
    outer, zero, one, two, weights,
):
    outer_kernel(
        forcing_ref, south_ref, north_ref, west_ref, east_ref, planes_ref, between_ref, large_ref,
        small_ref, outer, zero, one, two, weights,
    )
    lon_kernel(
        me_ref, inner_ref, outer, rate_ref, local_ref, edge_ref, lon_ref, lat_ref, lonc_ref, latc_ref
    )


def carries(received, coef_ref):
    ahead = jnp.zeros(received[0].shape[1:], jnp.float32)
    behind = ahead
    for k, ref in enumerate(received):
        ahead = ahead + coef_ref[6 * k + 4 : 6 * k + 5, :] * ref[0]
        behind = behind + coef_ref[6 * k + 5 : 6 * k + 6, :] * ref[1]
    return ahead, behind


def lat_kernel(local_ref, r0, r1, r2, r3, coef_ref, lon_ref, lat_ref, out_ref, edge_ref, plane, held_ref):
    ahead_in, behind_in = carries((r0, r1, r2, r3), coef_ref)

    def along_lon(x, carry):
        at = pl.multiple_of(x * YO, 8)
        plane[pl.ds(at, YO), :] = (
            local_ref[x]
            + lon_ref[2, pl.ds(x, 1), :] * ahead_in
            + lon_ref[3, pl.ds(x, 1), :] * behind_in
        )
        return carry

    lax.fori_loop(0, NX, along_lon, 0, unroll=2)
    held = jnp.zeros((NX, S), jnp.float32)
    for y in range(NY):
        held = lat_ref[0, y : y + 1, :] * held + lat_ref[1, y : y + 1, :] * plane[pl.ds(y, NX, stride=YO), :]
        held_ref[y] = held
    edge_ref[0, :NX, :] = held
    edge_ref[0, NX:, :] = jnp.zeros((YO - NX, S), jnp.float32)
    held = jnp.zeros((NX, S), jnp.float32)
    for y in range(NY - 1, -1, -1):
        quarter = lat_ref[1, y : y + 1, :]
        value = plane[pl.ds(y, NX, stride=YO), :]
        out_ref[pl.ds(y, NX, stride=YO), :] = quarter * (held_ref[y] + held)
        held = lat_ref[0, y : y + 1, :] * (quarter * value + held)
    edge_ref[1, :NX, :] = held
    edge_ref[1, NX:, :] = jnp.zeros((YO - NX, S), jnp.float32)


def finish_kernel(local_ref, r0, r1, r2, coef_ref, lat_ref, out_ref, carry_ref):
    carry_ref[0], carry_ref[1] = carries((r0, r1, r2), coef_ref)
    ahead, behind = lat_ref[2][:NY], lat_ref[3][:NY]

    for x in range(0, NX, 2):
        pair = [
            local_ref[i * YO : i * YO + NY, :]
            + ahead * carry_ref[0, i : i + 1, :]
            + behind * carry_ref[1, i : i + 1, :]
            for i in (x, x + 1)
        ]
        out_ref[x * NY : (x + 2) * NY, :] = jnp.concatenate(pair, 0).astype(jnp.bfloat16)


def update_kernel(control_ref, factor_ref, p0, p1, p2, p3, out_ref):
    for x in range(0, NX, 2):
        rows = slice(x * NY, (x + 2) * NY)
        total = factor_ref[0:1, :] * p0[rows, :].astype(jnp.float32)
        for k, ref in enumerate((p1, p2, p3)):
            total = total + factor_ref[k + 1 : k + 2, :] * ref[rows, :].astype(jnp.float32)
        for i in range(2):
            part = total[i * NY : (i + 1) * NY]
            out_ref[x + i] = (control_ref[x + i].astype(jnp.float32) - part).astype(jnp.bfloat16)


def call(kernel, outs, scratch=(), specs=None):
    def run(*operands):
        return built(len(operands))(*operands)

    def built(count):
        return pl.pallas_call(
        kernel,
        out_shape=outs,
        in_specs=specs or [VMEM] * count,
        scratch_shapes=list(scratch),
        compiler_params=pltpu.CompilerParams(vmem_limit_bytes=40 * 2**20),
    )

    return run


def in_place(*arrays):
    return [pltpu.with_memory_space_constraint(x, pltpu.MemorySpace.HBM) for x in arrays]


def f32(*shape):
    return jax.ShapeDtypeStruct(shape, jnp.float32)


def swap(x, axis, mask):
    return lax.ppermute(x, axis, [(i, i ^ mask) for i in range(lax.axis_size(axis))])


def three_parts(x):
    high = lax.reduce_precision(x, 8, 7)
    rest = x - high
    middle = lax.reduce_precision(rest, 8, 7)
    low = rest - middle
    return jnp.concatenate([high, middle, low], 0).astype(jnp.bfloat16)


def join_parts(parts):
    third = parts.shape[0] // 3
    parts = parts.astype(jnp.float32)
    return (parts[:third] + parts[third : 2 * third]) + parts[2 * third :]


def widen(coefs, before, after):
    return jnp.pad(coefs, ((0, 0), (before, after), (Y0 - 2, S - NY - 2 - Y0)))


def pack(cells, coefs):
    wide = jnp.pad(coefs, ((0, 0), (0, S - coefs.shape[1])))
    return jnp.concatenate([cells.reshape(-1, S), three_parts(wide)], 0)


def unpack(rows, n, m, w):
    return rows[: n * m].reshape(n, m, S), join_parts(rows[n * m :])[:, :w]


def fetch_kernel(
    lon_ref, lat_ref, cells_ref, transport_ref, reactivity_ref, out_ref, cells_out, coefs_out,
    lon_copy, lat_copy, transport_copy, reactivity_copy, rows, arrived,
):
    pairs = (
        (lon_ref, lon_copy),
        (lat_ref, lat_copy),
        (transport_ref, transport_copy),
        (reactivity_ref, reactivity_copy),
        (cells_ref, cells_out),
    )
    fetches = [pltpu.make_async_copy(a, b, arrived.at[i]) for i, (a, b) in enumerate(pairs)]
    for fetch in fetches:
        fetch.start()
    rows[...] = jnp.zeros_like(rows)
    for fetch in fetches[:2]:
        fetch.wait()
    for i in range(TI):
        rows[i : i + 1, :NX] = lon_copy[:, i * NX : (i + 1) * NX]
    for j in range(TJ):
        rows[TI + j : TI + j + 1, YO : YO + NY] = lat_copy[:, j * NY : (j + 1) * NY]
    parts, tiles = TI + TJ, TI * TJ
    values = rows[...]
    sums = lax.dot_general(
        jnp.ones((8, S), jnp.float32), values, (((1,), (1,)), ((), ())),
        precision=HIGHEST, preferred_element_type=jnp.float32,
    )
    part = lax.broadcasted_iota(jnp.int32, (parts, S), 0)
    place = (lax.broadcasted_iota(jnp.int32, (parts, S), 1) == part + 2 * YO).astype(jnp.float32)
    placed = jnp.dot(sums, place, precision=HIGHEST, preferred_element_type=jnp.float32)
    tile = lax.broadcasted_iota(jnp.int32, (tiles, parts), 0)
    part = lax.broadcasted_iota(jnp.int32, (tiles, parts), 1)
    pick = ((part == tile // TJ) | (part == tile % TJ + TI)).astype(jnp.float32)
    out_ref[...] = placed[:1] + jnp.dot(pick, values, precision=HIGHEST, preferred_element_type=jnp.float32)
    for fetch in fetches[2:]:
        fetch.wait()
    for f in range(FLD - 1):
        coefs_out[f] = transport_copy[f * NX : (f + 1) * NX, 0, :]
    coefs_out[FLD - 1] = reactivity_copy[:, 0, :]


def one_device(
    forcing, transport, reactivity, jacobian, pattern, lon_rate, lat_rate, vertical, step_scale, control
):
    tile = lax.axis_index("tile")
    tiles = TI * TJ
    anywhere = pl.BlockSpec(memory_space=pltpu.MemorySpace.HBM)
    sent, cells, coefs = call(
        fetch_kernel,
        (f32(tiles, S), jax.ShapeDtypeStruct((NX, NY, S), jnp.bfloat16), f32(FLD, NX, NY)),
        (
            pltpu.VMEM(lon_rate.shape, jnp.float32),
            pltpu.VMEM(lat_rate.shape, jnp.float32),
            pltpu.VMEM(((FLD - 1) * NX, 1, NY), jnp.float32),
            pltpu.VMEM((NX, 1, NY), jnp.float32),
            pltpu.VMEM((TI + TJ, S), jnp.float32),
            pltpu.SemaphoreType.DMA((5,)),
        ),
        specs=[anywhere] * 5,
    )(
        *in_place(
            lon_rate,
            lat_rate,
            forcing[0, 0],
            transport.reshape((FLD - 1) * NX, 1, NY),
            reactivity.reshape(NX, 1, NY),
        )
    )
    rates = lax.all_to_all(sent, "tile", split_axis=0, concat_axis=0, tiled=True)

    northward = pack(
        jnp.swapaxes(cells[:, NY - 3 :], 0, 1),
        jnp.swapaxes(coefs[:, :, NY - 2 :], 1, 2).reshape(2 * FLD, NX),
    )
    southward = pack(
        jnp.swapaxes(cells[:, :3], 0, 1), jnp.swapaxes(coefs[:, :, :2], 1, 2).reshape(2 * FLD, NX)
    )
    steps_up = [(i, i + 1) for i in range(tiles) if i % TJ < TJ - 1]
    from_south = lax.ppermute(northward, "tile", steps_up)
    from_north = lax.ppermute(southward, "tile", [(b, a) for a, b in steps_up])
    south, south_coefs = unpack(from_south, 3, NX, NX)
    north, north_coefs = unpack(from_north, 3, NX, NX)
    south_coefs = jnp.swapaxes(south_coefs.reshape(FLD, 2, NX), 1, 2)
    north_coefs = jnp.swapaxes(north_coefs.reshape(FLD, 2, NX), 1, 2)
    tall = jnp.concatenate([south_coefs, coefs, north_coefs], 2)

    def side(lines):
        return jnp.concatenate(
            [jnp.swapaxes(south[1:, lines], 0, 1), cells[lines], jnp.swapaxes(north[:2, lines], 0, 1)], 1
        )

    eastward = pack(side(slice(NX - 3, NX)), tall[:, NX - 2 :].reshape(2 * FLD, NY + 4))
    westward = pack(side(slice(0, 3)), tall[:, :2].reshape(2 * FLD, NY + 4))
    upper = (tile // TJ) % 2 == 1
    relayed = lax.ppermute(
        jnp.where(upper, eastward, westward),
        "tile",
        [(i, (i + (2 * TJ if i // TJ % 2 else -2 * TJ)) % tiles) for i in range(tiles)],
    )
    halves = swap(jnp.stack([jnp.where(upper, westward, eastward), relayed]), "tile", TJ)
    inner, between, large, small = call(
        inner_kernel,
        (
            f32(NX - 6, YO, S),
            f32(8, YP, S),
            jax.ShapeDtypeStruct((2 * S, 2 * S), jnp.bfloat16),
            jax.ShapeDtypeStruct((2 * S, S), jnp.bfloat16),
        ),
        (
            pltpu.VMEM((NX * YP, S), jnp.float32),
            pltpu.VMEM((NX * YP, S), jnp.float32),
            pltpu.VMEM((FLD, NX * YP, S), jnp.float32),
            pltpu.VMEM(pattern.shape, pattern.dtype),
            pltpu.VMEM((S, S), jnp.float32),
            pltpu.SemaphoreType.DMA((2,)),
        ),
        specs=[VMEM] * 4 + [anywhere] * 2,
    )(cells, south, north, widen(tall, 0, YP - NX), *in_place(pattern, jacobian[0]))
    from_west = jnp.where(upper, halves[0], halves[1])
    from_east = jnp.where(upper, halves[1], halves[0])
    west, west_coefs = unpack(from_west, 3, NY + 4, NY + 4)
    east, east_coefs = unpack(from_east, 3, NY + 4, NY + 4)
    planes = jnp.concatenate(
        [west_coefs.reshape(FLD, 2, NY + 4), tall, east_coefs.reshape(FLD, 2, NY + 4)], 1
    )
    planes = widen(planes, 1, YP - NX - 5)

    local, edge, lon, lat, lon_coef, lat_coef = call(
        outer_lon_kernel,
        (f32(NX, YO, S), f32(2, YO, S), f32(4, YO, S), f32(4, YO, S), f32(6 * 4, S), f32(6 * 3, S)),
        (pltpu.VMEM((6, YO, S), jnp.float32),)
        + tuple(pltpu.VMEM((12 * YP, S), jnp.float32) for _ in range(3))
        + (pltpu.VMEM((2, FLD, 5 * YP, S), jnp.float32),),
        specs=[pl.BlockSpec(memory_space=pltpu.SMEM)] + [VMEM] * 11,
    )(tile.reshape(1), cells, south, north, west, east, planes, between, large, small, inner, rates)

    def rounds(edge, coef, bits):
        received = []
        for k, mask in enumerate(bits):
            other = swap(edge, "tile", mask)
            received.append(other)
            if k + 1 < len(bits):
                mine = coef[6 * k : 6 * k + 2][:, None]
                theirs = coef[6 * k + 2 : 6 * k + 4][:, None]
                edge = mine * edge + theirs * other
        return received

    level_here = lax.axis_index("lev")
    mixing = lax.dynamic_index_in_dim(vertical, level_here, 1, keepdims=False).T
    factors = jnp.stack(
        [
            step_scale * lax.dynamic_index_in_dim(mixing, level_here ^ mask, 0, keepdims=False)
            for mask in range(4)
        ]
    )
    received = rounds(edge, lon_coef, LON_MASKS)
    received[0], factors = lax.optimization_barrier((received[0], factors))
    local, edge = call(
        lat_kernel,
        (f32(NX * YO, S), f32(2, YO, S)),
        (pltpu.VMEM((NX * YO, S), jnp.float32), pltpu.VMEM((NY, NX, S), jnp.float32)),
    )(local, *received, lon_coef, lon, lat)
    filtered = call(
        finish_kernel,
        jax.ShapeDtypeStruct((NX * NY, S), jnp.bfloat16),
        (pltpu.VMEM((2, YO, S), jnp.float32),),
    )(local, *rounds(edge, lat_coef, LAT_MASKS), lat_coef, lat)

    levels = [filtered, swap(filtered, "lev", 1), swap(filtered, "lev", 2)]
    levels.append(swap(levels[2], "lev", 1))
    updated = call(update_kernel, jax.ShapeDtypeStruct((NX, NY, S), jnp.bfloat16))(
        control[0, 0], factors, *levels
    )
    return updated[None, None]


def solution(mesh):
    in_specs = (
        P("lev", "tile", None, None, None),
        P(None, "lev", "tile", None, None),
        P("lev", "tile", None, None),
        P("lev", None, None),
        P(),
        P("tile", None),
        P("tile", None),
        P(),
        P(),
        P("lev", "tile", None, None, None),
    )
    out_specs = P("lev", "tile", None, None, None)
    return jax.shard_map(one_device, mesh=mesh, in_specs=in_specs, out_specs=out_specs, check_vma=False)
```

```python
import jax
import jax.numpy as jnp
from jax import lax
from jax.experimental import pallas as pl
from jax.experimental.pallas import tpu as pltpu
from jax.sharding import PartitionSpec as P

TJ = 8
TI = 16
STEPS = 3
NX = 36
NY = 36
S = 128
YP = 48
Y0 = 8
YO = 40
FLD = 5
HIGHEST = lax.Precision.HIGHEST
VMEM = pl.BlockSpec(memory_space=pltpu.VMEM)
LON_MASKS = (8, 16, 32, 64)
LAT_MASKS = (1, 2, 4)


def round_factors(me, sums, bits):
    tiles, rows = sums.shape[0], 6 * bits
    row = lax.broadcasted_iota(jnp.int32, (rows, tiles), 0)
    tile = lax.broadcasted_iota(jnp.int32, (rows, tiles), 1)
    level = jnp.zeros_like(row)
    for k in range(1, bits):
        level = level + (row >= 6 * k).astype(jnp.int32)
    kind = row - 6 * level
    here = jnp.full_like(row, me)
    block = lax.shift_right_logical(here, level)
    of_tile = lax.shift_right_logical(tile, level)
    upper = (block & 1) == 1
    own = of_tile == block
    other = of_tile == block + 1 - 2 * (block & 1)
    used = (
        ((kind == 0) & ~upper & other)
        | ((kind == 1) & upper & other)
        | ((kind == 2) & upper & own)
        | ((kind == 3) & ~upper & own)
        | ((kind == 4) & own & (tile < here))
        | ((kind == 5) & own & (tile > here))
    )
    total = jnp.dot(used.astype(jnp.float32), sums, precision=HIGHEST, preferred_element_type=jnp.float32)
    off = ((kind == 4) & ~upper) | ((kind == 5) & upper)
    gate = 1.0 - off.astype(jnp.float32)[:, :1]
    return gate * jnp.exp(-total)


def put_line(state, at, value):
    state[at : at + Y0, :] = jnp.zeros((Y0, S), jnp.float32)
    state[at + YP - 8 : at + YP, :] = jnp.zeros((8, S), jnp.float32)
    first = Y0 - (value.shape[0] - NY) // 2
    state[at + first : at + first + value.shape[0], :] = value


def put_rims(state, south_ref, north_ref, base, lines, skip):
    for j in range(3):
        for ref, row in ((south_ref, Y0 - 3 + j), (north_ref, Y0 + NY + j)):
            rim = ref[j][skip : skip + lines].astype(jnp.float32)
            state[pl.ds(base + row, lines, stride=YP), :] = rim


def put_weights(weights, planes_ref, first, lines):
    for f in range(FLD):
        column = planes_ref[f].T
        for x in range(lines):
            spread = jnp.broadcast_to(column[:YP, first + x : first + x + 1], (YP, S))
            weights[f, x * YP : (x + 1) * YP, :] = spread


def advance(source, weights, large, small, at, wat, lines):
    size = lines * YP
    here = source[at : at + size, :]
    west = source[at - YP : at - YP + size, :]
    east = source[at + YP : at + YP + size, :]
    south = pltpu.roll(here, 1, 0)
    north = pltpu.roll(here, size - 1, 0)
    moved = (
        here
        + weights[0, wat : wat + size, :] * (west - here)
        + weights[1, wat : wat + size, :] * (east - here)
        + weights[2, wat : wat + size, :] * (south - here)
        + weights[3, wat : wat + size, :] * (north - here)
    )
    m1, m2, m3 = split(moved)
    top = jnp.dot(jnp.concatenate([m1, m2], 1), large, preferred_element_type=jnp.float32)
    low = jnp.dot(jnp.concatenate([m3, m1], 1), small, preferred_element_type=jnp.float32)
    reacted = top[:, :S] + (top[:, S:] + low)
    return moved + weights[4, wat : wat + size, :] * reacted


def round_gradient(result, line):
    part = result[line * YP + Y0 : line * YP + Y0 + YO]
    return part.astype(jnp.bfloat16).astype(jnp.float32)


def inner_kernel(
    forcing_ref, south_ref, north_ref, planes_ref, pattern_ref, jacobian_ref,
    gradient_ref, between_ref, large_ref, small_ref,
    even, odd, weights, pattern_copy, jacobian_copy, arrived,
):
    fetches = [
        pltpu.make_async_copy(pattern_ref, pattern_copy, arrived.at[0]),
        pltpu.make_async_copy(jacobian_ref, jacobian_copy, arrived.at[1]),
    ]
    for fetch in fetches:
        fetch.start()
    for x in range(NX):
        put_line(even, x * YP, forcing_ref[x].astype(jnp.float32))
    put_rims(even, south_ref, north_ref, 0, NX, 0)
    put_weights(weights, planes_ref, 0, NX)

    for fetch in fetches:
        fetch.wait()
    blocks = pattern_copy.shape[0]
    spread = (
        lax.broadcasted_iota(jnp.int32, (blocks, S), 0)
        == lax.broadcasted_iota(jnp.int32, (blocks, S), 1) // (S // blocks)
    ).astype(jnp.float32)
    wide = jnp.dot(pattern_copy[...].astype(jnp.float32), spread, preferred_element_type=jnp.float32)
    mask = lax.dot_general(spread, wide, (((0,), (0,)), ((), ())), preferred_element_type=jnp.float32)
    w1, w2, w3 = split(jacobian_copy[...] * mask)
    both = jnp.concatenate([w1, w2], 1)
    large = jnp.concatenate([both, both], 0)
    small = jnp.concatenate([w1, w3], 0)
    large_ref[...] = large
    small_ref[...] = small

    source, target = even, odd
    for step in range(STEPS):
        first, last = 1 + step, NX - 1 - step
        groups = [(x, min(4, last - x)) for x in range(first, last, 4)]
        for x, lines in groups:
            result = advance(source, weights, large, small, x * YP, x * YP, lines)
            if step == STEPS - 1:
                for i in range(lines):
                    gradient_ref[x - 3 + i] = round_gradient(result, i)
            else:
                target[x * YP : (x + lines) * YP, :] = result
        if step < STEPS - 1:
            for i, x in enumerate((1 + step, 2 + step, NX - 3 - step, NX - 2 - step)):
                between_ref[4 * step + i] = target[x * YP : (x + 1) * YP, :]
        source, target = target, source


def outer_kernel(
    forcing_ref, south_ref, north_ref, west_ref, east_ref, planes_ref, between_ref, large_ref, small_ref,
    gradient_ref, zero, one, two, weights,
):
    large, small = large_ref[...], small_ref[...]
    slots = 6
    for side in range(2):
        base = side * slots * YP
        halo = (west_ref, east_ref)[side]
        for i in range(3):
            slot = i if side == 0 else i + 2
            put_line(zero, base + slot * YP, halo[i].astype(jnp.float32))
        first = 0 if side == 0 else NX - 2
        slot = 3 if side == 0 else 0
        for i in range(2):
            put_line(zero, base + (slot + i) * YP, forcing_ref[first + i].astype(jnp.float32))
        put_rims(zero, south_ref, north_ref, base + slot * YP, 2, first)
        put_weights(weights.at[side], planes_ref, 1 if side == 0 else NX, 5)

    def at(side, slot):
        return (side * slots + slot) * YP

    for side in range(2):
        done = advance(zero, weights.at[side], large, small, at(side, 1), 0 if side == 0 else 2 * YP, 3)
        for i in range(3):
            slot = i if side == 0 else i + 2
            one[at(side, slot) : at(side, slot + 1), :] = done[i * YP : (i + 1) * YP]
        for i in range(2):
            slot = i + 3 if side == 0 else i
            one[at(side, slot) : at(side, slot + 1), :] = between_ref[2 * side + i]
    for side in range(2):
        done = advance(one, weights.at[side], large, small, at(side, 1), YP, 3)
        for i in range(3):
            slot = i if side == 0 else i + 2
            two[at(side, slot) : at(side, slot + 1), :] = done[i * YP : (i + 1) * YP]
        for i in range(2):
            slot = i + 3 if side == 0 else i
            two[at(side, slot) : at(side, slot + 1), :] = between_ref[4 + 2 * side + i]
    for side in range(2):
        done = advance(two, weights.at[side], large, small, at(side, 1), 2 * YP if side == 0 else 0, 3)
        for i in range(3):
            gradient_ref[3 * side + i] = round_gradient(done, i)


def split(x):
    high = x.astype(jnp.bfloat16)
    rest = x - high.astype(jnp.float32)
    middle = rest.astype(jnp.bfloat16)
    return high, middle, (rest - middle.astype(jnp.float32)).astype(jnp.bfloat16)


def tables_kernel(me_ref, rate_ref, lon_ref, lat_ref, lonc_ref, latc_ref):
    fields = rate_ref[...].T
    row = lax.broadcasted_iota(jnp.int32, (YO, YO), 0)
    col = lax.broadcasted_iota(jnp.int32, (YO, YO), 1)
    upto = (col <= row).astype(jnp.float32)
    after = (col > row).astype(jnp.float32)
    for first, out in ((0, lon_ref), (YO, lat_ref)):
        rates = fields[first : first + YO]
        quarter = jnp.sqrt(jnp.sqrt(rates))
        before = jnp.dot(upto, rates, precision=HIGHEST, preferred_element_type=jnp.float32)
        beyond = jnp.dot(after, rates, precision=HIGHEST, preferred_element_type=jnp.float32)
        out[0] = jnp.exp(-rates)
        out[1] = quarter
        out[2] = quarter * jnp.exp(-before)
        out[3] = quarter * jnp.exp(-beyond)
    lonc_ref[...] = round_factors(me_ref[0] // TJ, fields[2 * YO : 2 * YO + TI], len(LON_MASKS))
    latc_ref[...] = round_factors(me_ref[0] % TJ, fields[2 * YO + TI : 2 * YO + TI + TJ], len(LAT_MASKS))


def lon_kernel(inner_ref, outer_ref, lon_ref, local_ref, edge_ref):
    def gradient(x):
        if x < 3:
            return outer_ref[x]
        return inner_ref[x - 3] if x < NX - 3 else outer_ref[x - NX + 6]

    held = jnp.zeros((YO, S), jnp.float32)
    for x in range(NX):
        held = lon_ref[0, x : x + 1, :] * held + lon_ref[1, x : x + 1, :] * gradient(x)
        local_ref[x] = held
    edge_ref[0] = held
    held = jnp.zeros((YO, S), jnp.float32)
    for x in range(NX - 1, -1, -1):
        quarter = lon_ref[1, x : x + 1, :]
        local_ref[x] = quarter * (local_ref[x] + held)
        held = lon_ref[0, x : x + 1, :] * (quarter * gradient(x) + held)
    edge_ref[1] = held


def outer_lon_kernel(
    forcing_ref, south_ref, north_ref, west_ref, east_ref, planes_ref, between_ref, large_ref,
    small_ref, inner_ref, lon_ref, local_ref, edge_ref, outer, zero, one, two, weights,
):
    outer_kernel(
        forcing_ref, south_ref, north_ref, west_ref, east_ref, planes_ref, between_ref, large_ref,
        small_ref, outer, zero, one, two, weights,
    )
    lon_kernel(inner_ref, outer, lon_ref, local_ref, edge_ref)


def carries(received, coef_ref):
    ahead = jnp.zeros(received[0].shape[1:], jnp.float32)
    behind = ahead
    for k, ref in enumerate(received):
        ahead = ahead + coef_ref[6 * k + 4 : 6 * k + 5, :] * ref[0]
        behind = behind + coef_ref[6 * k + 5 : 6 * k + 6, :] * ref[1]
    return ahead, behind


def lat_kernel(local_ref, r0, r1, r2, r3, coef_ref, lon_ref, lat_ref, out_ref, edge_ref, plane, held_ref):
    ahead_in, behind_in = carries((r0, r1, r2, r3), coef_ref)

    def along_lon(x, carry):
        at = pl.multiple_of(x * YO, 8)
        plane[pl.ds(at, YO), :] = (
            local_ref[x]
            + lon_ref[2, pl.ds(x, 1), :] * ahead_in
            + lon_ref[3, pl.ds(x, 1), :] * behind_in
        )
        return carry

    lax.fori_loop(0, NX, along_lon, 0, unroll=2)
    held = jnp.zeros((NX, S), jnp.float32)
    for y in range(NY):
        held = lat_ref[0, y : y + 1, :] * held + lat_ref[1, y : y + 1, :] * plane[pl.ds(y, NX, stride=YO), :]
        held_ref[y] = held
    edge_ref[0, :NX, :] = held
    edge_ref[0, NX:, :] = jnp.zeros((YO - NX, S), jnp.float32)
    held = jnp.zeros((NX, S), jnp.float32)
    for y in range(NY - 1, -1, -1):
        quarter = lat_ref[1, y : y + 1, :]
        value = plane[pl.ds(y, NX, stride=YO), :]
        out_ref[pl.ds(y, NX, stride=YO), :] = quarter * (held_ref[y] + held)
        held = lat_ref[0, y : y + 1, :] * (quarter * value + held)
    edge_ref[1, :NX, :] = held
    edge_ref[1, NX:, :] = jnp.zeros((YO - NX, S), jnp.float32)


def finish_kernel(local_ref, r0, r1, r2, coef_ref, lat_ref, out_ref, carry_ref):
    carry_ref[0], carry_ref[1] = carries((r0, r1, r2), coef_ref)
    ahead, behind = lat_ref[2][:NY], lat_ref[3][:NY]

    for x in range(0, NX, 2):
        pair = [
            local_ref[i * YO : i * YO + NY, :]
            + ahead * carry_ref[0, i : i + 1, :]
            + behind * carry_ref[1, i : i + 1, :]
            for i in (x, x + 1)
        ]
        out_ref[x * NY : (x + 2) * NY, :] = jnp.concatenate(pair, 0).astype(jnp.bfloat16)


def update_kernel(control_ref, factor_ref, p0, p1, p2, p3, out_ref):
    for x in range(0, NX, 2):
        rows = slice(x * NY, (x + 2) * NY)
        total = factor_ref[0:1, :] * p0[rows, :].astype(jnp.float32)
        for k, ref in enumerate((p1, p2, p3)):
            total = total + factor_ref[k + 1 : k + 2, :] * ref[rows, :].astype(jnp.float32)
        for i in range(2):
            part = total[i * NY : (i + 1) * NY]
            out_ref[x + i] = (control_ref[x + i].astype(jnp.float32) - part).astype(jnp.bfloat16)


def call(kernel, outs, scratch=(), specs=None):
    def run(*operands):
        return built(len(operands))(*operands)

    def built(count):
        return pl.pallas_call(
        kernel,
        out_shape=outs,
        in_specs=specs or [VMEM] * count,
        scratch_shapes=list(scratch),
        compiler_params=pltpu.CompilerParams(vmem_limit_bytes=40 * 2**20),
    )

    return run


def in_place(*arrays):
    return [pltpu.with_memory_space_constraint(x, pltpu.MemorySpace.HBM) for x in arrays]


def f32(*shape):
    return jax.ShapeDtypeStruct(shape, jnp.float32)


def swap(x, axis, mask):
    return lax.ppermute(x, axis, [(i, i ^ mask) for i in range(lax.axis_size(axis))])


def three_parts(x):
    high = lax.reduce_precision(x, 8, 7)
    rest = x - high
    middle = lax.reduce_precision(rest, 8, 7)
    low = rest - middle
    return jnp.concatenate([high, middle, low], 0).astype(jnp.bfloat16)


def join_parts(parts):
    third = parts.shape[0] // 3
    parts = parts.astype(jnp.float32)
    return (parts[:third] + parts[third : 2 * third]) + parts[2 * third :]


def widen(coefs, before, after):
    return jnp.pad(coefs, ((0, 0), (before, after), (Y0 - 2, S - NY - 2 - Y0)))


def pack(cells, coefs):
    wide = jnp.pad(coefs, ((0, 0), (0, S - coefs.shape[1])))
    return jnp.concatenate([cells.reshape(-1, S), three_parts(wide)], 0)


def unpack(rows, n, m, w):
    return rows[: n * m].reshape(n, m, S), join_parts(rows[n * m :])[:, :w]


def fetch_kernel(
    lon_ref, lat_ref, cells_ref, transport_ref, reactivity_ref, lon_out, lat_out, cells_out, coefs_out,
    transport_copy, reactivity_copy, arrived,
):
    pairs = (
        (transport_ref, transport_copy.at[: (FLD - 1) * NX]),
        (reactivity_ref, reactivity_copy.at[:NX]),
        (cells_ref, cells_out),
        (lon_ref, lon_out),
        (lat_ref, lat_out),
    )
    fetches = [pltpu.make_async_copy(a, b, arrived.at[i]) for i, (a, b) in enumerate(pairs)]
    for fetch in fetches:
        fetch.start()
    for fetch in fetches:
        fetch.wait()
    for f in range(FLD - 1):
        coefs_out[f] = transport_copy[f * NX : (f + 1) * NX, 0, :]
    coefs_out[FLD - 1] = reactivity_copy[:NX, 0, :]


def rows_kernel(lon_ref, lat_ref, out_ref, rows):
    rows[...] = jnp.zeros_like(rows)
    for i in range(TI):
        rows[i : i + 1, :NX] = lon_ref[:, i * NX : (i + 1) * NX]
    for j in range(TJ):
        rows[TI + j : TI + j + 1, YO : YO + NY] = lat_ref[:, j * NY : (j + 1) * NY]
    parts, tiles = TI + TJ, TI * TJ
    values = rows[...]
    sums = lax.dot_general(
        jnp.ones((8, S), jnp.float32), values, (((1,), (1,)), ((), ())),
        precision=HIGHEST, preferred_element_type=jnp.float32,
    )
    part = lax.broadcasted_iota(jnp.int32, (parts, S), 0)
    place = (lax.broadcasted_iota(jnp.int32, (parts, S), 1) == part + 2 * YO).astype(jnp.float32)
    placed = jnp.dot(sums, place, precision=HIGHEST, preferred_element_type=jnp.float32)
    tile = lax.broadcasted_iota(jnp.int32, (tiles, parts), 0)
    part = lax.broadcasted_iota(jnp.int32, (tiles, parts), 1)
    pick = ((part == tile // TJ) | (part == tile % TJ + TI)).astype(jnp.float32)
    out_ref[...] = placed[:1] + jnp.dot(pick, values, precision=HIGHEST, preferred_element_type=jnp.float32)


def one_device(
    forcing, transport, reactivity, jacobian, pattern, lon_rate, lat_rate, vertical, step_scale, control
):
    tile = lax.axis_index("tile")
    tiles = TI * TJ
    anywhere = pl.BlockSpec(memory_space=pltpu.MemorySpace.HBM)
    lon_here, lat_here, cells, coefs = call(
        fetch_kernel,
        (
            f32(*lon_rate.shape),
            f32(*lat_rate.shape),
            jax.ShapeDtypeStruct((NX, NY, S), jnp.bfloat16),
            f32(FLD, NX, NY),
        ),
        (
            pltpu.VMEM(((FLD - 1) * NX + 8, 1, NY), jnp.float32),
            pltpu.VMEM((NX + 8, 1, NY), jnp.float32),
            pltpu.SemaphoreType.DMA((5,)),
        ),
        specs=[anywhere] * 5,
    )(
        *in_place(
            lon_rate,
            lat_rate,
            forcing[0, 0],
            transport.reshape((FLD - 1) * NX, 1, NY),
            reactivity.reshape(NX, 1, NY),
        )
    )
    sent = call(rows_kernel, f32(tiles, S), (pltpu.VMEM((TI + TJ, S), jnp.float32),))(lon_here, lat_here)
    rates = lax.all_to_all(sent, "tile", split_axis=0, concat_axis=0, tiled=True)

    northward = pack(
        jnp.swapaxes(cells[:, NY - 3 :], 0, 1),
        jnp.swapaxes(coefs[:, :, NY - 2 :], 1, 2).reshape(2 * FLD, NX),
    )
    southward = pack(
        jnp.swapaxes(cells[:, :3], 0, 1), jnp.swapaxes(coefs[:, :, :2], 1, 2).reshape(2 * FLD, NX)
    )
    steps_up = [(i, i + 1) for i in range(tiles) if i % TJ < TJ - 1]
    from_south = lax.ppermute(northward, "tile", steps_up)
    from_north = lax.ppermute(southward, "tile", [(b, a) for a, b in steps_up])
    south, south_coefs = unpack(from_south, 3, NX, NX)
    north, north_coefs = unpack(from_north, 3, NX, NX)
    south_coefs = jnp.swapaxes(south_coefs.reshape(FLD, 2, NX), 1, 2)
    north_coefs = jnp.swapaxes(north_coefs.reshape(FLD, 2, NX), 1, 2)
    tall = jnp.concatenate([south_coefs, coefs, north_coefs], 2)

    def side(lines):
        return jnp.concatenate(
            [jnp.swapaxes(south[1:, lines], 0, 1), cells[lines], jnp.swapaxes(north[:2, lines], 0, 1)], 1
        )

    eastward = pack(side(slice(NX - 3, NX)), tall[:, NX - 2 :].reshape(2 * FLD, NY + 4))
    westward = pack(side(slice(0, 3)), tall[:, :2].reshape(2 * FLD, NY + 4))
    upper = (tile // TJ) % 2 == 1
    relayed = lax.ppermute(
        jnp.where(upper, eastward, westward),
        "tile",
        [(i, (i + (2 * TJ if i // TJ % 2 else -2 * TJ)) % tiles) for i in range(tiles)],
    )
    halves = swap(jnp.stack([jnp.where(upper, westward, eastward), relayed]), "tile", TJ)
    inner, between, large, small = call(
        inner_kernel,
        (
            f32(NX - 6, YO, S),
            f32(8, YP, S),
            jax.ShapeDtypeStruct((2 * S, 2 * S), jnp.bfloat16),
            jax.ShapeDtypeStruct((2 * S, S), jnp.bfloat16),
        ),
        (
            pltpu.VMEM((YO * YP, S), jnp.float32),
            pltpu.VMEM((YO * YP, S), jnp.float32),
            pltpu.VMEM((FLD, NX * YP, S), jnp.float32),
            pltpu.VMEM(pattern.shape, pattern.dtype),
            pltpu.VMEM((S, S), jnp.float32),
            pltpu.SemaphoreType.DMA((2,)),
        ),
        specs=[VMEM] * 4 + [anywhere] * 2,
    )(cells, south, north, widen(tall, 0, YP - NX), *in_place(pattern, jacobian[0]))
    from_west = jnp.where(upper, halves[0], halves[1])
    from_east = jnp.where(upper, halves[1], halves[0])
    west, west_coefs = unpack(from_west, 3, NY + 4, NY + 4)
    east, east_coefs = unpack(from_east, 3, NY + 4, NY + 4)
    planes = jnp.concatenate(
        [west_coefs.reshape(FLD, 2, NY + 4), tall, east_coefs.reshape(FLD, 2, NY + 4)], 1
    )
    planes = widen(planes, 1, YP - NX - 5)

    lon, lat, lon_coef, lat_coef = call(
        tables_kernel,
        (f32(4, YO, S), f32(4, YO, S), f32(6 * 4, S), f32(6 * 3, S)),
        specs=[pl.BlockSpec(memory_space=pltpu.SMEM), VMEM],
    )(tile.reshape(1), rates)
    local, edge = call(
        outer_lon_kernel,
        (f32(NX, YO, S), f32(2, YO, S)),
        (pltpu.VMEM((6, YO, S), jnp.float32),)
        + tuple(pltpu.VMEM((16 * YP, S), jnp.float32) for _ in range(3))
        + (pltpu.VMEM((2, FLD, 5 * YP, S), jnp.float32),),
    )(cells, south, north, west, east, planes, between, large, small, inner, lon)

    def rounds(edge, coef, bits):
        received = []
        for k, mask in enumerate(bits):
            other = swap(edge, "tile", mask)
            received.append(other)
            if k + 1 < len(bits):
                mine = coef[6 * k : 6 * k + 2][:, None]
                theirs = coef[6 * k + 2 : 6 * k + 4][:, None]
                edge = mine * edge + theirs * other
        return received

    level_here = lax.axis_index("lev")
    mixing = lax.dynamic_index_in_dim(vertical, level_here, 1, keepdims=False).T
    factors = jnp.stack(
        [
            step_scale * lax.dynamic_index_in_dim(mixing, level_here ^ mask, 0, keepdims=False)
            for mask in range(4)
        ]
    )
    received = rounds(edge, lon_coef, LON_MASKS)
    received[0], factors = lax.optimization_barrier((received[0], factors))
    local, edge = call(
        lat_kernel,
        (f32(YO * YO, S), f32(2, YO, S)),
        (pltpu.VMEM((YO * YO, S), jnp.float32), pltpu.VMEM((NY, NX, S), jnp.float32)),
    )(local, *received, lon_coef, lon, lat)
    filtered = call(
        finish_kernel,
        jax.ShapeDtypeStruct((NX * NY, S), jnp.bfloat16),
        (pltpu.VMEM((2, YO, S), jnp.float32),),
    )(local, *rounds(edge, lat_coef, LAT_MASKS), lat_coef, lat)

    levels = [filtered, swap(filtered, "lev", 1), swap(filtered, "lev", 2)]
    levels.append(swap(levels[2], "lev", 1))
    updated = call(update_kernel, jax.ShapeDtypeStruct((NX, NY, S), jnp.bfloat16))(
        control[0, 0], factors, *levels
    )
    return updated[None, None]


def solution(mesh):
    in_specs = (
        P("lev", "tile", None, None, None),
        P(None, "lev", "tile", None, None),
        P("lev", "tile", None, None),
        P("lev", None, None),
        P(),
        P("tile", None),
        P("tile", None),
        P(),
        P(),
        P("lev", "tile", None, None, None),
    )
    out_specs = P("lev", "tile", None, None, None)
    return jax.shard_map(one_device, mesh=mesh, in_specs=in_specs, out_specs=out_specs, check_vma=False)
```

```python
import jax
import jax.numpy as jnp
from jax import lax
from jax.experimental import pallas as pl
from jax.experimental.pallas import tpu as pltpu
from jax.sharding import PartitionSpec as P

TJ = 8
TI = 16
STEPS = 3
NX = 36
NY = 36
S = 128
YP = 48
Y0 = 8
YO = 40
FLD = 5
HIGHEST = lax.Precision.HIGHEST
VMEM = pl.BlockSpec(memory_space=pltpu.VMEM)
LON_MASKS = (8, 16, 32, 64)
LAT_MASKS = (1, 2, 4)


def round_factors(me, sums, bits):
    tiles, rows = sums.shape[0], 6 * bits
    row = lax.broadcasted_iota(jnp.int32, (rows, tiles), 0)
    tile = lax.broadcasted_iota(jnp.int32, (rows, tiles), 1)
    level = jnp.zeros_like(row)
    for k in range(1, bits):
        level = level + (row >= 6 * k).astype(jnp.int32)
    kind = row - 6 * level
    here = jnp.full_like(row, me)
    block = lax.shift_right_logical(here, level)
    of_tile = lax.shift_right_logical(tile, level)
    upper = (block & 1) == 1
    own = of_tile == block
    other = of_tile == block + 1 - 2 * (block & 1)
    used = (
        ((kind == 0) & ~upper & other)
        | ((kind == 1) & upper & other)
        | ((kind == 2) & upper & own)
        | ((kind == 3) & ~upper & own)
        | ((kind == 4) & own & (tile < here))
        | ((kind == 5) & own & (tile > here))
    )
    total = jnp.dot(used.astype(jnp.float32), sums, precision=HIGHEST, preferred_element_type=jnp.float32)
    off = ((kind == 4) & ~upper) | ((kind == 5) & upper)
    gate = 1.0 - off.astype(jnp.float32)[:, :1]
    return gate * jnp.exp(-total)


def put_line(state, at, value):
    state[at : at + Y0, :] = jnp.zeros((Y0, S), jnp.float32)
    state[at + YP - 8 : at + YP, :] = jnp.zeros((8, S), jnp.float32)
    first = Y0 - (value.shape[0] - NY) // 2
    state[at + first : at + first + value.shape[0], :] = value


def put_rims(state, south_ref, north_ref, base, lines, skip):
    for j in range(3):
        for ref, row in ((south_ref, Y0 - 3 + j), (north_ref, Y0 + NY + j)):
            rim = ref[j][skip : skip + lines].astype(jnp.float32)
            state[pl.ds(base + row, lines, stride=YP), :] = rim


def put_weights(weights, planes_ref, first, lines):
    for f in range(FLD):
        column = planes_ref[f].T
        for x in range(lines):
            spread = jnp.broadcast_to(column[:YP, first + x : first + x + 1], (YP, S))
            weights[f, x * YP : (x + 1) * YP, :] = spread


def advance(source, weights, large, small, at, wat, lines):
    size = lines * YP
    here = source[at : at + size, :]
    west = source[at - YP : at - YP + size, :]
    east = source[at + YP : at + YP + size, :]
    south = pltpu.roll(here, 1, 0)
    north = pltpu.roll(here, size - 1, 0)
    moved = (
        here
        + weights[0, wat : wat + size, :] * (west - here)
        + weights[1, wat : wat + size, :] * (east - here)
        + weights[2, wat : wat + size, :] * (south - here)
        + weights[3, wat : wat + size, :] * (north - here)
    )
    m1, m2, m3 = split(moved)
    top = jnp.dot(jnp.concatenate([m1, m2], 1), large, preferred_element_type=jnp.float32)
    low = jnp.dot(jnp.concatenate([m3, m1], 1), small, preferred_element_type=jnp.float32)
    reacted = top[:, :S] + (top[:, S:] + low)
    return moved + weights[4, wat : wat + size, :] * reacted


def round_gradient(result, line):
    part = result[line * YP + Y0 : line * YP + Y0 + YO]
    return part.astype(jnp.bfloat16).astype(jnp.float32)


def inner_kernel(
    forcing_ref, south_ref, north_ref, planes_ref, pattern_ref, jacobian_ref,
    gradient_ref, between_ref, large_ref, small_ref,
    even, odd, weights, pattern_copy, jacobian_copy, arrived,
):
    fetches = [
        pltpu.make_async_copy(pattern_ref, pattern_copy, arrived.at[0]),
        pltpu.make_async_copy(jacobian_ref, jacobian_copy, arrived.at[1]),
    ]
    for fetch in fetches:
        fetch.start()
    for x in range(NX):
        put_line(even, x * YP, forcing_ref[x].astype(jnp.float32))
    put_rims(even, south_ref, north_ref, 0, NX, 0)
    put_weights(weights, planes_ref, 0, NX)

    for fetch in fetches:
        fetch.wait()
    blocks = pattern_copy.shape[0]
    spread = (
        lax.broadcasted_iota(jnp.int32, (blocks, S), 0)
        == lax.broadcasted_iota(jnp.int32, (blocks, S), 1) // (S // blocks)
    ).astype(jnp.float32)
    wide = jnp.dot(pattern_copy[...].astype(jnp.float32), spread, preferred_element_type=jnp.float32)
    mask = lax.dot_general(spread, wide, (((0,), (0,)), ((), ())), preferred_element_type=jnp.float32)
    w1, w2, w3 = split(jacobian_copy[...] * mask)
    both = jnp.concatenate([w1, w2], 1)
    large = jnp.concatenate([both, both], 0)
    small = jnp.concatenate([w1, w3], 0)
    large_ref[...] = large
    small_ref[...] = small

    source, target = even, odd
    for step in range(STEPS):
        first, last = 1 + step, NX - 1 - step
        groups = [(x, min(4, last - x)) for x in range(first, last, 4)]
        for x, lines in groups:
            result = advance(source, weights, large, small, x * YP, x * YP, lines)
            if step == STEPS - 1:
                for i in range(lines):
                    gradient_ref[x - 3 + i] = round_gradient(result, i)
            else:
                target[x * YP : (x + lines) * YP, :] = result
        if step < STEPS - 1:
            for i, x in enumerate((1 + step, 2 + step, NX - 3 - step, NX - 2 - step)):
                between_ref[4 * step + i] = target[x * YP : (x + 1) * YP, :]
        source, target = target, source


def outer_kernel(
    forcing_ref, south_ref, north_ref, west_ref, east_ref, planes_ref, between_ref, large_ref, small_ref,
    gradient_ref, zero, one, two, weights,
):
    large, small = large_ref[...], small_ref[...]
    slots = 6
    for side in range(2):
        base = side * slots * YP
        halo = (west_ref, east_ref)[side]
        for i in range(3):
            slot = i if side == 0 else i + 2
            put_line(zero, base + slot * YP, halo[i].astype(jnp.float32))
        first = 0 if side == 0 else NX - 2
        slot = 3 if side == 0 else 0
        for i in range(2):
            put_line(zero, base + (slot + i) * YP, forcing_ref[first + i].astype(jnp.float32))
        put_rims(zero, south_ref, north_ref, base + slot * YP, 2, first)
        put_weights(weights.at[side], planes_ref, 1 if side == 0 else NX, 5)

    def at(side, slot):
        return (side * slots + slot) * YP

    for side in range(2):
        done = advance(zero, weights.at[side], large, small, at(side, 1), 0 if side == 0 else 2 * YP, 3)
        for i in range(3):
            slot = i if side == 0 else i + 2
            one[at(side, slot) : at(side, slot + 1), :] = done[i * YP : (i + 1) * YP]
        for i in range(2):
            slot = i + 3 if side == 0 else i
            one[at(side, slot) : at(side, slot + 1), :] = between_ref[2 * side + i]
    for side in range(2):
        done = advance(one, weights.at[side], large, small, at(side, 1), YP, 3)
        for i in range(3):
            slot = i if side == 0 else i + 2
            two[at(side, slot) : at(side, slot + 1), :] = done[i * YP : (i + 1) * YP]
        for i in range(2):
            slot = i + 3 if side == 0 else i
            two[at(side, slot) : at(side, slot + 1), :] = between_ref[4 + 2 * side + i]
    for side in range(2):
        done = advance(two, weights.at[side], large, small, at(side, 1), 2 * YP if side == 0 else 0, 3)
        for i in range(3):
            gradient_ref[3 * side + i] = round_gradient(done, i)


def split(x):
    high = x.astype(jnp.bfloat16)
    rest = x - high.astype(jnp.float32)
    middle = rest.astype(jnp.bfloat16)
    return high, middle, (rest - middle.astype(jnp.float32)).astype(jnp.bfloat16)


def tables_kernel(me_ref, rate_ref, lon_ref, lat_ref, lonc_ref, latc_ref):
    fields = rate_ref[...].T
    row = lax.broadcasted_iota(jnp.int32, (YO, YO), 0)
    col = lax.broadcasted_iota(jnp.int32, (YO, YO), 1)
    upto = (col <= row).astype(jnp.float32)
    after = (col > row).astype(jnp.float32)
    for first, out in ((0, lon_ref), (YO, lat_ref)):
        rates = fields[first : first + YO]
        quarter = jnp.sqrt(jnp.sqrt(rates))
        before = jnp.dot(upto, rates, precision=HIGHEST, preferred_element_type=jnp.float32)
        beyond = jnp.dot(after, rates, precision=HIGHEST, preferred_element_type=jnp.float32)
        out[0] = jnp.exp(-rates)
        out[1] = quarter
        out[2] = quarter * jnp.exp(-before)
        out[3] = quarter * jnp.exp(-beyond)
    lonc_ref[...] = round_factors(me_ref[0] // TJ, fields[2 * YO : 2 * YO + TI], len(LON_MASKS))
    latc_ref[...] = round_factors(me_ref[0] % TJ, fields[2 * YO + TI : 2 * YO + TI + TJ], len(LAT_MASKS))


def lon_kernel(inner_ref, outer_ref, lon_ref, local_ref, edge_ref):
    def gradient(x):
        if x < 3:
            return outer_ref[x]
        return inner_ref[x - 3] if x < NX - 3 else outer_ref[x - NX + 6]

    held = jnp.zeros((YO, S), jnp.float32)
    for x in range(NX):
        held = lon_ref[0, x : x + 1, :] * held + lon_ref[1, x : x + 1, :] * gradient(x)
        local_ref[x] = held
    edge_ref[0] = held
    held = jnp.zeros((YO, S), jnp.float32)
    for x in range(NX - 1, -1, -1):
        quarter = lon_ref[1, x : x + 1, :]
        local_ref[x] = quarter * (local_ref[x] + held)
        held = lon_ref[0, x : x + 1, :] * (quarter * gradient(x) + held)
    edge_ref[1] = held


def outer_lon_kernel(
    forcing_ref, south_ref, north_ref, west_ref, east_ref, planes_ref, between_ref, large_ref,
    small_ref, inner_ref, lon_ref, local_ref, edge_ref, outer, zero, one, two, weights,
):
    outer_kernel(
        forcing_ref, south_ref, north_ref, west_ref, east_ref, planes_ref, between_ref, large_ref,
        small_ref, outer, zero, one, two, weights,
    )
    lon_kernel(inner_ref, outer, lon_ref, local_ref, edge_ref)


def carries(received, coef_ref):
    ahead = jnp.zeros(received[0].shape[1:], jnp.float32)
    behind = ahead
    for k, ref in enumerate(received):
        ahead = ahead + coef_ref[6 * k + 4 : 6 * k + 5, :] * ref[0]
        behind = behind + coef_ref[6 * k + 5 : 6 * k + 6, :] * ref[1]
    return ahead, behind


def lat_kernel(local_ref, r0, r1, r2, r3, coef_ref, lon_ref, lat_ref, out_ref, edge_ref, plane, held_ref):
    ahead_in, behind_in = carries((r0, r1, r2, r3), coef_ref)

    def along_lon(x, carry):
        at = pl.multiple_of(x * YO, 8)
        plane[pl.ds(at, YO), :] = (
            local_ref[x]
            + lon_ref[2, pl.ds(x, 1), :] * ahead_in
            + lon_ref[3, pl.ds(x, 1), :] * behind_in
        )
        return carry

    lax.fori_loop(0, NX, along_lon, 0, unroll=2)
    held = jnp.zeros((NX, S), jnp.float32)
    for y in range(NY):
        held = lat_ref[0, y : y + 1, :] * held + lat_ref[1, y : y + 1, :] * plane[pl.ds(y, NX, stride=YO), :]
        held_ref[y] = held
    edge_ref[0, :NX, :] = held
    edge_ref[0, NX:, :] = jnp.zeros((YO - NX, S), jnp.float32)
    held = jnp.zeros((NX, S), jnp.float32)
    for y in range(NY - 1, -1, -1):
        quarter = lat_ref[1, y : y + 1, :]
        value = plane[pl.ds(y, NX, stride=YO), :]
        out_ref[pl.ds(y, NX, stride=YO), :] = quarter * (held_ref[y] + held)
        held = lat_ref[0, y : y + 1, :] * (quarter * value + held)
    edge_ref[1, :NX, :] = held
    edge_ref[1, NX:, :] = jnp.zeros((YO - NX, S), jnp.float32)


def finish_kernel(local_ref, r0, r1, r2, coef_ref, lat_ref, out_ref, carry_ref):
    carry_ref[0], carry_ref[1] = carries((r0, r1, r2), coef_ref)
    ahead, behind = lat_ref[2][:NY], lat_ref[3][:NY]

    for x in range(0, NX, 2):
        pair = [
            local_ref[i * YO : i * YO + NY, :]
            + ahead * carry_ref[0, i : i + 1, :]
            + behind * carry_ref[1, i : i + 1, :]
            for i in (x, x + 1)
        ]
        out_ref[x * NY : (x + 2) * NY, :] = jnp.concatenate(pair, 0).astype(jnp.bfloat16)


def update_kernel(control_ref, factor_ref, p0, p1, p2, p3, out_ref):
    for x in range(0, NX, 2):
        rows = slice(x * NY, (x + 2) * NY)
        total = factor_ref[0:1, :] * p0[rows, :].astype(jnp.float32)
        for k, ref in enumerate((p1, p2, p3)):
            total = total + factor_ref[k + 1 : k + 2, :] * ref[rows, :].astype(jnp.float32)
        for i in range(2):
            part = total[i * NY : (i + 1) * NY]
            out_ref[x + i] = (control_ref[x + i].astype(jnp.float32) - part).astype(jnp.bfloat16)


def call(kernel, outs, scratch=(), specs=None):
    def run(*operands):
        return built(len(operands))(*operands)

    def built(count):
        return pl.pallas_call(
        kernel,
        out_shape=outs,
        in_specs=specs or [VMEM] * count,
        scratch_shapes=list(scratch),
        compiler_params=pltpu.CompilerParams(vmem_limit_bytes=40 * 2**20),
    )

    return run


def in_place(*arrays):
    return [pltpu.with_memory_space_constraint(x, pltpu.MemorySpace.HBM) for x in arrays]


def f32(*shape):
    return jax.ShapeDtypeStruct(shape, jnp.float32)


def swap(x, axis, mask):
    return lax.ppermute(x, axis, [(i, i ^ mask) for i in range(lax.axis_size(axis))])


def three_parts(x):
    high = lax.reduce_precision(x, 8, 7)
    rest = x - high
    middle = lax.reduce_precision(rest, 8, 7)
    low = rest - middle
    return jnp.concatenate([high, middle, low], 1).astype(jnp.bfloat16)


def join_parts(parts, w):
    parts = parts.astype(jnp.float32)
    return (parts[:, :w] + parts[:, w : 2 * w]) + parts[:, 2 * w : 3 * w]


def widen(coefs, before, after):
    return jnp.pad(coefs, ((0, 0), (before, after), (Y0 - 2, S - NY - 2 - Y0)))


def pack(cells, coefs):
    parts = three_parts(coefs)
    wide = jnp.pad(parts, ((0, 0), (0, S - parts.shape[1])))
    return jnp.concatenate([cells.reshape(-1, S), wide], 0)


def unpack(rows, n, m, w):
    return rows[: n * m].reshape(n, m, S), join_parts(rows[n * m :], w)


def fetch_kernel(
    lon_ref, lat_ref, cells_ref, transport_ref, reactivity_ref, lon_out, lat_out, cells_out, coefs_out,
    transport_copy, reactivity_copy, arrived,
):
    pairs = (
        (transport_ref, transport_copy.at[: (FLD - 1) * NX]),
        (reactivity_ref, reactivity_copy.at[:NX]),
        (cells_ref, cells_out),
        (lon_ref, lon_out),
        (lat_ref, lat_out),
    )
    fetches = [pltpu.make_async_copy(a, b, arrived.at[i]) for i, (a, b) in enumerate(pairs)]
    for fetch in fetches:
        fetch.start()
    for fetch in fetches:
        fetch.wait()
    for f in range(FLD - 1):
        coefs_out[f] = transport_copy[f * NX : (f + 1) * NX, 0, :]
    coefs_out[FLD - 1] = reactivity_copy[:NX, 0, :]


def rows_kernel(lon_ref, lat_ref, out_ref, rows):
    rows[...] = jnp.zeros_like(rows)
    for i in range(TI):
        rows[i : i + 1, :NX] = lon_ref[:, i * NX : (i + 1) * NX]
    for j in range(TJ):
        rows[TI + j : TI + j + 1, YO : YO + NY] = lat_ref[:, j * NY : (j + 1) * NY]
    parts, tiles = TI + TJ, TI * TJ
    values = rows[...]
    sums = lax.dot_general(
        jnp.ones((8, S), jnp.float32), values, (((1,), (1,)), ((), ())),
        precision=HIGHEST, preferred_element_type=jnp.float32,
    )
    part = lax.broadcasted_iota(jnp.int32, (parts, S), 0)
    place = (lax.broadcasted_iota(jnp.int32, (parts, S), 1) == part + 2 * YO).astype(jnp.float32)
    placed = jnp.dot(sums, place, precision=HIGHEST, preferred_element_type=jnp.float32)
    tile = lax.broadcasted_iota(jnp.int32, (tiles, parts), 0)
    part = lax.broadcasted_iota(jnp.int32, (tiles, parts), 1)
    pick = ((part == tile // TJ) | (part == tile % TJ + TI)).astype(jnp.float32)
    out_ref[...] = placed[:1] + jnp.dot(pick, values, precision=HIGHEST, preferred_element_type=jnp.float32)


def one_device(
    forcing, transport, reactivity, jacobian, pattern, lon_rate, lat_rate, vertical, step_scale, control
):
    tile = lax.axis_index("tile")
    tiles = TI * TJ
    anywhere = pl.BlockSpec(memory_space=pltpu.MemorySpace.HBM)
    lon_here, lat_here, cells, coefs = call(
        fetch_kernel,
        (
            f32(*lon_rate.shape),
            f32(*lat_rate.shape),
            jax.ShapeDtypeStruct((NX, NY, S), jnp.bfloat16),
            f32(FLD, NX, NY),
        ),
        (
            pltpu.VMEM(((FLD - 1) * NX + 8, 1, NY), jnp.float32),
            pltpu.VMEM((NX + 8, 1, NY), jnp.float32),
            pltpu.SemaphoreType.DMA((5,)),
        ),
        specs=[anywhere] * 5,
    )(
        *in_place(
            lon_rate,
            lat_rate,
            forcing[0, 0],
            transport.reshape((FLD - 1) * NX, 1, NY),
            reactivity.reshape(NX, 1, NY),
        )
    )
    sent = call(rows_kernel, f32(tiles, S), (pltpu.VMEM((TI + TJ, S), jnp.float32),))(lon_here, lat_here)
    rates = lax.all_to_all(sent, "tile", split_axis=0, concat_axis=0, tiled=True)

    northward = pack(
        jnp.swapaxes(cells[:, NY - 3 :], 0, 1),
        jnp.swapaxes(coefs[:, :, NY - 2 :], 1, 2).reshape(2 * FLD, NX),
    )
    southward = pack(
        jnp.swapaxes(cells[:, :3], 0, 1), jnp.swapaxes(coefs[:, :, :2], 1, 2).reshape(2 * FLD, NX)
    )
    steps_up = [(i, i + 1) for i in range(tiles) if i % TJ < TJ - 1]
    from_south = lax.ppermute(northward, "tile", steps_up)
    from_north = lax.ppermute(southward, "tile", [(b, a) for a, b in steps_up])
    south, south_coefs = unpack(from_south, 3, NX, NX)
    north, north_coefs = unpack(from_north, 3, NX, NX)
    south_coefs = jnp.swapaxes(south_coefs.reshape(FLD, 2, NX), 1, 2)
    north_coefs = jnp.swapaxes(north_coefs.reshape(FLD, 2, NX), 1, 2)
    tall = jnp.concatenate([south_coefs, coefs, north_coefs], 2)

    def side(lines):
        return jnp.concatenate(
            [jnp.swapaxes(south[1:, lines], 0, 1), cells[lines], jnp.swapaxes(north[:2, lines], 0, 1)], 1
        )

    eastward = pack(side(slice(NX - 3, NX)), tall[:, NX - 2 :].reshape(2 * FLD, NY + 4))
    westward = pack(side(slice(0, 3)), tall[:, :2].reshape(2 * FLD, NY + 4))
    upper = (tile // TJ) % 2 == 1
    relayed = lax.ppermute(
        jnp.where(upper, eastward, westward),
        "tile",
        [(i, (i + (2 * TJ if i // TJ % 2 else -2 * TJ)) % tiles) for i in range(tiles)],
    )
    halves = swap(jnp.stack([jnp.where(upper, westward, eastward), relayed]), "tile", TJ)
    inner, between, large, small = call(
        inner_kernel,
        (
            f32(NX - 6, YO, S),
            f32(8, YP, S),
            jax.ShapeDtypeStruct((2 * S, 2 * S), jnp.bfloat16),
            jax.ShapeDtypeStruct((2 * S, S), jnp.bfloat16),
        ),
        (
            pltpu.VMEM((YO * YP, S), jnp.float32),
            pltpu.VMEM((YO * YP, S), jnp.float32),
            pltpu.VMEM((FLD, NX * YP, S), jnp.float32),
            pltpu.VMEM(pattern.shape, pattern.dtype),
            pltpu.VMEM((S, S), jnp.float32),
            pltpu.SemaphoreType.DMA((2,)),
        ),
        specs=[VMEM] * 4 + [anywhere] * 2,
    )(cells, south, north, widen(tall, 0, YP - NX), *in_place(pattern, jacobian[0]))
    from_west = jnp.where(upper, halves[0], halves[1])
    from_east = jnp.where(upper, halves[1], halves[0])
    west, west_coefs = unpack(from_west, 3, NY + 4, NY + 4)
    east, east_coefs = unpack(from_east, 3, NY + 4, NY + 4)
    planes = jnp.concatenate(
        [west_coefs.reshape(FLD, 2, NY + 4), tall, east_coefs.reshape(FLD, 2, NY + 4)], 1
    )
    planes = widen(planes, 1, YP - NX - 5)

    lon, lat, lon_coef, lat_coef = call(
        tables_kernel,
        (f32(4, YO, S), f32(4, YO, S), f32(6 * 4, S), f32(6 * 3, S)),
        specs=[pl.BlockSpec(memory_space=pltpu.SMEM), VMEM],
    )(tile.reshape(1), rates)
    local, edge = call(
        outer_lon_kernel,
        (f32(NX, YO, S), f32(2, YO, S)),
        (pltpu.VMEM((6, YO, S), jnp.float32),)
        + tuple(pltpu.VMEM((16 * YP, S), jnp.float32) for _ in range(3))
        + (pltpu.VMEM((2, FLD, 5 * YP, S), jnp.float32),),
    )(cells, south, north, west, east, planes, between, large, small, inner, lon)

    def rounds(edge, coef, bits):
        received = []
        for k, mask in enumerate(bits):
            other = swap(edge, "tile", mask)
            received.append(other)
            if k + 1 < len(bits):
                mine = coef[6 * k : 6 * k + 2][:, None]
                theirs = coef[6 * k + 2 : 6 * k + 4][:, None]
                edge = mine * edge + theirs * other
        return received

    level_here = lax.axis_index("lev")
    mixing = lax.dynamic_index_in_dim(vertical, level_here, 1, keepdims=False).T
    factors = jnp.stack(
        [
            step_scale * lax.dynamic_index_in_dim(mixing, level_here ^ mask, 0, keepdims=False)
            for mask in range(4)
        ]
    )
    received = rounds(edge, lon_coef, LON_MASKS)
    received[0], factors = lax.optimization_barrier((received[0], factors))
    local, edge = call(
        lat_kernel,
        (f32(YO * YO, S), f32(2, YO, S)),
        (pltpu.VMEM((YO * YO, S), jnp.float32), pltpu.VMEM((NY, NX, S), jnp.float32)),
    )(local, *received, lon_coef, lon, lat)
    filtered = call(
        finish_kernel,
        jax.ShapeDtypeStruct((NX * NY, S), jnp.bfloat16),
        (pltpu.VMEM((2, YO, S), jnp.float32),),
    )(local, *rounds(edge, lat_coef, LAT_MASKS), lat_coef, lat)

    levels = [filtered, swap(filtered, "lev", 1), swap(filtered, "lev", 2)]
    levels.append(swap(levels[2], "lev", 1))
    updated = call(update_kernel, jax.ShapeDtypeStruct((NX, NY, S), jnp.bfloat16))(
        control[0, 0], factors, *levels
    )
    return updated[None, None]


def solution(mesh):
    in_specs = (
        P("lev", "tile", None, None, None),
        P(None, "lev", "tile", None, None),
        P("lev", "tile", None, None),
        P("lev", None, None),
        P(),
        P("tile", None),
        P("tile", None),
        P(),
        P(),
        P("lev", "tile", None, None, None),
    )
    out_specs = P("lev", "tile", None, None, None)
    return jax.shard_map(one_device, mesh=mesh, in_specs=in_specs, out_specs=out_specs, check_vma=False)
```
